32 devices in a mesh: kcol: 8 (over y, x, core), ion: 4 (over z).
Axes of the slice: x: 2, y: 2, z: 4, core: 2. Of those that a mesh axis runs over, the one named last changes fastest.
Arguments:
- ions: float32 [4, 81920], P(None, ('kcol', 'ion')), may hold values from -1.5 to 1.5, as said below
- col_ids: int32 [1024], P('kcol'), may hold values from 0 to 4095, as said below
Outputs:
- ion_forces: float32 [4, 81920], P(None, ('kcol', 'ion'))
- energy: float32 [], replicated
The draws below stay inside these ranges and needn't reach their ends.
Inputs may be any that keep to these rules, and one draw needn't show every extreme that they name: `col_ids`: distinct column numbers. `ions`: rows 0 to 2 lie in [0, 1); row 3 has magnitudes 0.5 to 1.5.
All inputs are finite; a program needn't handle non-finite values.
Results may differ from the reference program's by a relative error of at most 0.0003.
Values sent between devices are 32-bit elements; how exact they have to be, the bound alone decides.
No kernel may reach another device: no remote copies, remote signals or barrier semaphores. Data moves between devices by JAX's collectives and lax.ppermute only.
A program may use at most 64 MiB of HBM per device.

```python
import math
import jax
import jax.numpy as jnp
from jax import lax

KX = 32
ION_DEV = 2560
COLUMNS = 1024
TOTAL_IONS = 81920


def draw_ions(key, part):
    key_pos = jax.random.fold_in(key, 11)
    key_mag = jax.random.fold_in(key, 12)
    key_sign = jax.random.fold_in(key, 13)
    coords = jax.random.uniform(key_pos, (3, TOTAL_IONS), jnp.float32, 0.0, 1.0)
    signs = jnp.where(jax.random.bernoulli(key_sign, 0.5, (TOTAL_IONS,)), 1.0, -1.0).astype(jnp.float32)
    magnitude = jax.random.uniform(key_mag, (TOTAL_IONS,), jnp.float32, 0.5, 1.5)
    charges = signs * magnitude
    return jnp.concatenate([coords, charges[None, :]], 0).astype(jnp.float32)


def draw_col_ids(key, part):
    order = jax.random.permutation(jax.random.fold_in(key, 21), jnp.arange(4096, dtype=jnp.int32))
    return order[:COLUMNS].astype(jnp.int32)


def setup_inputs(seed: int = 0) -> dict:
    keys = jax.random.split(jax.random.key(seed), 3)
    return {
        "ions": draw_ions(jax.random.fold_in(keys[2], 71), 0),
        "col_ids": draw_col_ids(jax.random.fold_in(keys[2], 71), 0),
    }


def wave_numbers(col_ids):
    wave_x = jnp.arange(KX, dtype=jnp.int32)
    wave_y = col_ids // 64 - 32
    wave_z = col_ids % 64 - 32
    return (wave_x, wave_y, wave_z)

def kspace_weight(wave_x, wave_y, wave_z):
    radial = wave_y * wave_y + wave_z * wave_z
    along = wave_x * wave_x
    squared = along[:, None] + radial[None, :]
    inside = (squared <= 1024) & (squared > 0)
    squared_f = squared.astype(jnp.float32)
    halving = jnp.where(wave_x == 0, jnp.float32(0.5), jnp.float32(1.0))[:, None]
    return jnp.where(inside, halving * jnp.exp(-squared_f / 1600.0) / jnp.maximum(squared_f, 1.0), jnp.float32(0.0))

def phase_tables(block, wave_x, wave_y, wave_z):
    two_pi = 2.0 * math.pi
    angle_x = two_pi * wave_x.astype(jnp.float32)[:, None] * block[0][None, :]
    angle_yz = two_pi * (wave_y.astype(jnp.float32)[:, None] * block[1][None, :] + wave_z.astype(jnp.float32)[:, None] * block[2][None, :])
    return (jnp.cos(angle_x), jnp.sin(angle_x), jnp.cos(angle_yz), jnp.sin(angle_yz))

def factor_piece(block, waves):
    cos_x, sin_x, cos_yz, sin_yz = phase_tables(block, *waves)
    charge = block[3][None, :]
    left = jnp.concatenate([charge * cos_x, charge * sin_x], 0)
    right = jnp.concatenate([cos_yz, sin_yz], 0)
    product = lax.dot_general(left, right, (((1,), (1,)), ((), ())), precision=lax.Precision.HIGHEST, preferred_element_type=jnp.float32)
    nwave = cos_x.shape[0]
    ncol = cos_yz.shape[0]
    real_part = product[:nwave, :ncol] - product[nwave:, ncol:]
    imag_part = product[:nwave, ncol:] + product[nwave:, :ncol]
    return jnp.stack([real_part, imag_part])

def combine_matrix(weight, factor, wave_x):
    g_real = weight * factor[0]
    g_imag = -weight * factor[1]
    scaled = wave_x.astype(jnp.float32)[:, None]
    x_real = scaled * g_real
    x_imag = scaled * g_imag
    return jnp.concatenate([jnp.concatenate([g_real.T, -g_imag.T], 1), jnp.concatenate([g_imag.T, g_real.T], 1), jnp.concatenate([x_real.T, -x_imag.T], 1), jnp.concatenate([x_imag.T, x_real.T], 1)], 0)

def force_piece(block, combined, waves, force_scale, potential_scale):
    cos_x, sin_x, cos_yz, sin_yz = phase_tables(block, *waves)
    basis = jnp.concatenate([cos_x, sin_x], 0)
    spread = jnp.dot(combined, basis, precision=lax.Precision.HIGHEST, preferred_element_type=jnp.float32)
    ncol = cos_yz.shape[0]
    h_real0 = spread[:ncol]
    h_imag0 = spread[ncol:2 * ncol]
    h_real1 = spread[2 * ncol:3 * ncol]
    h_imag1 = spread[3 * ncol:]
    imag_zero = h_real0 * sin_yz + h_imag0 * cos_yz
    real_zero = h_real0 * cos_yz - h_imag0 * sin_yz
    imag_one = h_real1 * sin_yz + h_imag1 * cos_yz
    charge = block[3]
    wave_y = waves[1].astype(jnp.float32)[:, None]
    wave_z = waves[2].astype(jnp.float32)[:, None]
    force_x = force_scale * charge * lax.optimization_barrier(jnp.sum(imag_one, 0))
    force_y = force_scale * charge * lax.optimization_barrier(jnp.sum(wave_y * imag_zero, 0))
    force_z = force_scale * charge * lax.optimization_barrier(jnp.sum(wave_z * imag_zero, 0))
    potential = potential_scale * lax.optimization_barrier(jnp.sum(real_zero, 0))
    return jnp.stack([force_x, force_y, force_z, potential])

def reference(ions, col_ids):
    waves = wave_numbers(col_ids)
    weight = kspace_weight(*waves)
    blocks = ions.reshape(4, -1, ION_DEV).transpose(1, 0, 2)

    def add_factor(total, block):
        return (total + factor_piece(block, waves), None)
    factor, unused = lax.scan(add_factor, jnp.zeros((2, KX, COLUMNS), jnp.float32), blocks)
    energy = jnp.float32(0.01 / TOTAL_IONS) * jnp.sum(weight * (factor[0] * factor[0] + factor[1] * factor[1]))
    combined = combine_matrix(weight, factor, waves[0])
    force_scale = jnp.float32(0.04 * math.pi / math.sqrt(TOTAL_IONS))
    potential_scale = jnp.float32(0.4 / math.sqrt(TOTAL_IONS))
    pieces = lax.map(lambda block: force_piece(block, combined, waves, force_scale, potential_scale), blocks)
    ion_forces = pieces.transpose(1, 0, 2).reshape(4, TOTAL_IONS)
    return (ion_forces, energy)
```

```python
import functools
import math

import jax
import jax.numpy as jnp
from jax import lax
from jax.experimental import pallas as pl
from jax.experimental.pallas import tpu as pltpu
from jax.sharding import PartitionSpec as P

KX = 32
SPAN = 64
LANES = 128
TILE = 256
COS_COEFFS = (
    0.9999992107823219,
    -19.738980355764017,
    64.92865742103359,
    -85.27162153430098,
    58.790492120130835,
    -21.07110562763074,
)


def cos_turns(turns):
    rest = turns - jnp.round(turns)
    square = rest * rest
    value = jnp.float32(COS_COEFFS[-1])
    for coeff in COS_COEFFS[-2::-1]:
        value = value * square + jnp.float32(coeff)
    return value


def split(value):
    high = value.astype(jnp.bfloat16)
    low = (value - high.astype(jnp.float32)).astype(jnp.bfloat16)
    return high, low


def lane_iota(rows):
    return lax.broadcasted_iota(jnp.int32, (rows, LANES), 1)


def column_of(block, row):
    return jnp.broadcast_to(block.T[:, row : row + 1], (LANES, LANES))


def fill_yz_tables(ions8_ref, table_ref):
    lane = lane_iota(LANES)
    wave = (lane % SPAN - SPAN // 2).astype(jnp.float32)
    shift = jnp.where(lane < SPAN, jnp.float32(0.0), jnp.float32(-0.25))

    def body(b, carry):
        base = pl.multiple_of(b * LANES, LANES)
        block = ions8_ref[:, pl.ds(base, LANES)]
        table_ref[pl.ds(base, LANES), :LANES] = cos_turns(column_of(block, 1) * wave + shift)
        table_ref[pl.ds(base, LANES), LANES:] = cos_turns(column_of(block, 2) * wave + shift)
        return carry

    lax.fori_loop(0, table_ref.shape[0] // LANES, body, 0)


def columns_block(table_ref, pick_ref, start, rows):
    y_part = table_ref[start : start + rows, :LANES]
    z_part = table_ref[start : start + rows, LANES:]

    def take(part, row):
        pick = jnp.broadcast_to(pick_ref[0, row : row + 1, :], (rows, LANES))
        return jnp.take_along_axis(part, pick, axis=1, mode="promise_in_bounds")

    cos_y, sin_y = take(y_part, 0), take(y_part, 1)
    cos_z, sin_z = take(z_part, 2), take(z_part, 3)
    return cos_y * cos_z - sin_y * sin_z, sin_y * cos_z + cos_y * sin_z


def fill_columns(table_ref, pick_ref, start, high_ref, low_ref, rows=64):
    for r in range(start, start + TILE, rows):
        cos_part, sin_part = columns_block(table_ref, pick_ref, r, rows)
        high_ref[r : r + rows, :LANES], low_ref[r : r + rows, :LANES] = split(cos_part)
        high_ref[r : r + rows, LANES:], low_ref[r : r + rows, LANES:] = split(sin_part)


def dot(a, b, dims=((1,), (0,))):
    return lax.dot_general(a, b, (dims, ((), ())), preferred_element_type=jnp.float32)


def factor_kernel(ions8_ref, pick_ref, out_ref, table_ref, left_ref, high_ref, low_ref):
    count = ions8_ref.shape[1]

    @pl.when(pl.program_id(0) == 0)
    def _():
        fill_yz_tables(ions8_ref, table_ref)
        wave = lax.broadcasted_iota(jnp.int32, (2 * KX, LANES), 0)
        shift = jnp.where(wave < KX, jnp.float32(0.0), jnp.float32(-0.25))
        wave = (wave % KX).astype(jnp.float32)

        def body(b, carry):
            at = pl.ds(pl.multiple_of(b * LANES, LANES), LANES)
            value = ions8_ref[3:4, at] * cos_turns(wave * ions8_ref[0:1, at] + shift)
            left_ref[: 2 * KX, at], left_ref[2 * KX :, at] = split(value)
            return carry

        lax.fori_loop(0, count // LANES, body, 0)

    total_high = jnp.zeros((4 * KX, 2 * LANES), jnp.float32)
    total_low = jnp.zeros((2 * KX, 2 * LANES), jnp.float32)
    for start in range(0, count, TILE):
        fill_columns(table_ref, pick_ref, start, high_ref, low_ref)
        left = left_ref[:, start : start + TILE]
        total_high += dot(left, high_ref[start : start + TILE, :])
        total_low += dot(left[: 2 * KX], low_ref[start : start + TILE, :])
    product = total_high[: 2 * KX] + total_high[2 * KX :] + total_low
    out_ref[0, :KX, :] = product[:KX, :LANES] - product[KX:, LANES:]
    out_ref[0, KX:, :] = product[:KX, LANES:] + product[KX:, :LANES]


def force_kernel(
    ions8_ref, pick_ref, wave_ref, factor_ref, out_ref, energy_ref, table_ref, high_ref, low_ref, sum_ref,
    *, force_scale, potential_scale,
):
    count = ions8_ref.shape[1]
    group = pl.program_id(0)

    @pl.when(group == 0)
    def _():
        fill_yz_tables(ions8_ref, table_ref)
        sum_ref[...] = jnp.zeros_like(sum_ref)

    wave_x = lax.broadcasted_iota(jnp.int32, (KX, LANES), 0)
    wave_y = jnp.broadcast_to(wave_ref[0, 0:1, :], (KX, LANES))
    wave_z = jnp.broadcast_to(wave_ref[0, 1:2, :], (KX, LANES))
    squared = wave_x * wave_x + (wave_y * wave_y + wave_z * wave_z)
    inside = (squared <= 1024) & (squared > 0)
    squared_f = squared.astype(jnp.float32)
    halving = jnp.where(wave_x == 0, jnp.float32(0.5), jnp.float32(1.0))
    weight = jnp.where(
        inside,
        halving * jnp.exp(-squared_f / 1600.0) / jnp.maximum(squared_f, 1.0),
        jnp.float32(0.0),
    )
    real = factor_ref[0, :KX, :]
    imag = factor_ref[0, KX:, :]
    energy_ref[0] = jnp.sum((weight * (real * real + imag * imag)).reshape(KX // 8, 8, LANES), 0)
    g_real = weight * real
    g_imag = -weight * imag
    base = jnp.concatenate(
        [jnp.concatenate([g_real, -g_imag], 1), jnp.concatenate([g_imag, g_real], 1)], 0
    )
    scale_x = (lax.broadcasted_iota(jnp.int32, (2 * KX, 1), 0) % KX).astype(jnp.float32)
    scale_y = jnp.concatenate([wave_ref[0, 0:1, :]] * 2, 1).astype(jnp.float32)
    scale_z = jnp.concatenate([wave_ref[0, 1:2, :]] * 2, 1).astype(jnp.float32)
    mix = jnp.concatenate([base, base * scale_y, base * scale_z, base * scale_x], 0)
    mix_high, mix_low = split(mix)
    nt = ((1,), (1,))
    for start in range(0, count, TILE):
        fill_columns(table_ref, pick_ref, start, high_ref, low_ref)
        high = high_ref[start : start + TILE, :]
        low = low_ref[start : start + TILE, :]
        sum_ref[start : start + TILE, :] += dot(high, mix_high, nt) + dot(high, mix_low, nt) + dot(low, mix_high, nt)

    @pl.when(group == pl.num_programs(0) - 1)
    def _():
        lane = lane_iota(LANES)
        wave = (lane % KX).astype(jnp.float32)
        quarter = lane // KX
        shift = jnp.where(quarter == 1, 0.25, jnp.where(quarter == 2, -0.25, 0.0)).astype(jnp.float32)
        row = lax.broadcasted_iota(jnp.int32, (8, 2 * LANES), 0)
        col = lax.broadcasted_iota(jnp.int32, (8, 2 * LANES), 1) // (2 * KX)
        pick = (row < 4) & (col == jnp.where(row == 0, 3, jnp.where(row == 3, 0, row)))
        pick = jnp.where(pick, 1.0, 0.0).astype(jnp.bfloat16)

        def body(b, carry):
            at = pl.ds(pl.multiple_of(b * LANES, LANES), LANES)
            phase = cos_turns(column_of(ions8_ref[:, at], 0) * wave + shift)
            other = jnp.where(lane < 2 * KX, pltpu.roll(phase, 2 * KX, 1), phase)
            value = sum_ref[at, :] * jnp.concatenate([phase, other], 1)
            value_high, value_low = split(value)
            sums = dot(pick, value_high, nt) + dot(pick, value_low, nt)
            charge = ions8_ref[3:4, at]
            out_ref[0:3, at] = sums[0:3] * (charge * jnp.float32(force_scale))
            out_ref[3:4, at] = sums[3:4] * jnp.float32(potential_scale)
            return carry

        lax.fori_loop(0, count // LANES, body, 0)


def tree_sum(parts):
    while len(parts) > 1:
        parts = [parts[i] + parts[i + 1] for i in range(0, len(parts), 2)]
    return parts[0]


def flip(value, axis, step):
    size = lax.axis_size(axis)
    return lax.ppermute(value, axis, [(i, i ^ step) for i in range(size)])


def swap_groups(value, step):
    return jnp.concatenate([value[i ^ step][None] for i in range(value.shape[0])], 0)


def per_device(ions, col_ids):
    groups = lax.axis_size("kcol")
    rows = lax.axis_size("ion")
    count = ions.shape[1]
    total = count * groups * rows
    cols = col_ids[None]
    step = 1
    while step < groups:
        cols = jnp.concatenate([cols, flip(cols, "kcol", step)], 0)
        step *= 2
    wave_y = cols // SPAN - SPAN // 2
    wave_z = cols % SPAN - SPAN // 2
    pick = jnp.stack([wave_y + SPAN // 2, wave_y + 3 * SPAN // 2, wave_z + SPAN // 2, wave_z + 3 * SPAN // 2], 1)
    waves = jnp.stack([wave_y, wave_z], 1)
    ions8 = jnp.concatenate([ions, jnp.zeros_like(ions)], 0)

    ions_spec = pl.BlockSpec((8, count), lambda g: (0, 0))
    pick_spec = pl.BlockSpec((1, 4, LANES), lambda g: (g, 0, 0))
    wave_spec = pl.BlockSpec((1, 2, LANES), lambda g: (g, 0, 0))
    factor_spec = pl.BlockSpec((1, 2 * KX, LANES), lambda g: (g, 0, 0))
    halves = [pltpu.VMEM((count, 2 * LANES), jnp.bfloat16)] * 2
    partial_factor = pl.pallas_call(
        factor_kernel,
        grid=(groups,),
        in_specs=[ions_spec, pick_spec],
        out_specs=factor_spec,
        out_shape=jax.ShapeDtypeStruct((groups, 2 * KX, LANES), jnp.float32),
        scratch_shapes=[
            pltpu.VMEM((count, 2 * LANES), jnp.float32),
            pltpu.VMEM((4 * KX, count), jnp.bfloat16),
            *halves,
        ],
        name="factor",
    )(ions8, pick)

    pairs = partial_factor.reshape(groups // 2, 2, 2 * KX, LANES)
    kept = pairs[:, 0] + flip(pairs[:, 1], "kcol", 1)
    step = 2
    while step < groups:
        kept = kept + swap_groups(flip(kept, "kcol", step), step // 2)
        step *= 2
    step = 1
    while step < rows:
        kept = kept + flip(kept, "ion", step)
        step *= 2
    factor = jnp.stack([kept, flip(kept, "kcol", 1)], 1).reshape(groups, 2 * KX, LANES)

    forces, energy_parts = pl.pallas_call(
        functools.partial(
            force_kernel,
            force_scale=0.04 * math.pi / math.sqrt(total),
            potential_scale=0.4 / math.sqrt(total),
        ),
        grid=(groups,),
        in_specs=[ions_spec, pick_spec, wave_spec, factor_spec],
        out_specs=[pl.BlockSpec((4, count), lambda g: (0, 0)), pl.BlockSpec((1, 8, LANES), lambda g: (g, 0, 0))],
        out_shape=[
            jax.ShapeDtypeStruct((4, count), jnp.float32),
            jax.ShapeDtypeStruct((groups, 8, LANES), jnp.float32),
        ],
        scratch_shapes=[
            pltpu.VMEM((count, 2 * LANES), jnp.float32),
            *halves,
            pltpu.VMEM((count, 2 * LANES), jnp.float32),
        ],
        name="force",
    )(ions8, pick, waves, factor)
    energy = jnp.float32(0.01 / total) * jnp.sum(tree_sum([energy_parts[i] for i in range(groups)]))
    return (forces, energy)


def solution(mesh):
    return jax.shard_map(
        per_device,
        mesh=mesh,
        in_specs=(P(None, ("kcol", "ion")), P("kcol")),
        out_specs=(P(None, ("kcol", "ion")), P()),
        check_vma=False,
    )
```

```python
import functools
import math

import jax
import jax.numpy as jnp
from jax import lax
from jax.experimental import pallas as pl
from jax.experimental.pallas import tpu as pltpu
from jax.sharding import PartitionSpec as P

KX = 32
SPAN = 64
HALF = SPAN // 2
LANES = 128
TILE = 256
NT = ((1,), (1,))
NN = ((1,), (0,))
SIN_COEFFS = (3.1415902702069918, -5.167406733272337, 2.5440105185033337, -0.5594624554679438)
COS_COEFFS = (0.9999999532476085, -4.934792830619664, 4.058411352862771, -1.3318765680813944, 0.21968961109803095)


def horner(coeffs, square):
    value = jnp.float32(coeffs[-1])
    for coeff in coeffs[-2::-1]:
        value = value * square + jnp.float32(coeff)
    return value


def cos_sin_turns(turns):
    rest = turns - jnp.round(turns)
    square = rest * rest
    sin_half = rest * horner(SIN_COEFFS, square)
    cos_half = horner(COS_COEFFS, square)
    twice = sin_half + sin_half
    return 1.0 - twice * sin_half, twice * cos_half


def split(value):
    high = value.astype(jnp.bfloat16)
    low = (value - high.astype(jnp.float32)).astype(jnp.bfloat16)
    return high, low


def dot(a, b, dims):
    return lax.dot_general(a, b, (dims, ((), ())), preferred_element_type=jnp.float32)


def row_starts(rows):
    return sorted({*range(0, rows - 7, 8), rows - 8})


def table_kernel(ions_ref, cos_y, sin_y, cos_z, sin_z, basis_ref, left_ref, coord_ref):
    count = ions_ref.shape[1]
    rows = count // LANES
    for s in range(rows):
        at = slice(s * LANES, (s + 1) * LANES)
        coord_ref[0, s : s + 1, :] = ions_ref[1:2, at]
        coord_ref[1, s : s + 1, :] = ions_ref[2:3, at]

    def fill(m, carry):
        wave = m.astype(jnp.float32)
        for axis, (cos_ref, sin_ref) in enumerate(((cos_y, sin_y), (cos_z, sin_z))):
            cos_part, sin_part = cos_sin_turns(coord_ref[axis] * wave)
            up = pl.ds((HALF + m) * rows, rows)
            down = pl.ds((HALF - m) * rows, rows)
            cos_ref[up, :] = cos_part
            sin_ref[up, :] = sin_part
            cos_ref[down, :] = cos_part
            sin_ref[down, :] = -sin_part
        return carry

    lax.fori_loop(0, HALF + 1, fill, 0)
    wave_x = lax.broadcasted_iota(jnp.int32, (KX, LANES), 0).astype(jnp.float32)

    def body(b, carry):
        at = pl.ds(pl.multiple_of(b * LANES, LANES), LANES)
        cos_part, sin_part = cos_sin_turns(wave_x * ions_ref[0:1, at])
        basis_ref[:KX, at] = cos_part
        basis_ref[KX:, at] = sin_part
        charge = ions_ref[3:4, at]
        left_ref[:KX, at], left_ref[2 * KX : 3 * KX, at] = split(charge * cos_part)
        left_ref[KX : 2 * KX, at], left_ref[3 * KX :, at] = split(charge * sin_part)
        return carry

    lax.fori_loop(0, rows, body, 0)


def factor_kernel(pick_ref, cos_y, sin_y, cos_z, sin_z, left_ref, out_ref, high_ref, low_ref, cos_ref, sin_ref):
    rows = left_ref.shape[1] // LANES

    def column(c, carry):
        at_y = pick_ref[0, 0, c]
        at_z = pick_ref[0, 1, c]
        for start in row_starts(rows):
            y_at = pl.ds(at_y + start, 8)
            z_at = pl.ds(at_z + start, 8)
            cy, sy, cz, sz = cos_y[y_at, :], sin_y[y_at, :], cos_z[z_at, :], sin_z[z_at, :]
            at = pl.ds(c * rows + start, 8)
            cos_ref[at, :] = cy * cz - sy * sz
            sin_ref[at, :] = sy * cz + cy * sz
        return carry

    lax.fori_loop(0, LANES, column, 0, unroll=8)
    total_high = jnp.zeros((4 * KX, 2 * LANES), jnp.float32)
    total_low = jnp.zeros((2 * KX, 2 * LANES), jnp.float32)
    for tile in range(rows // 2):
        for s in (2 * tile, 2 * tile + 1):
            at = pl.ds(s, LANES, stride=rows)
            high_ref[0, s, :LANES, :], low_ref[0, s, :LANES, :] = split(cos_ref[at, :])
            high_ref[0, s, LANES:, :], low_ref[0, s, LANES:, :] = split(sin_ref[at, :])
        high = jnp.concatenate([high_ref[0, 2 * tile], high_ref[0, 2 * tile + 1]], 1)
        low = jnp.concatenate([low_ref[0, 2 * tile], low_ref[0, 2 * tile + 1]], 1)
        left = left_ref[:, tile * TILE : (tile + 1) * TILE]
        total_high += dot(left, high, NT)
        total_low += dot(left[: 2 * KX], low, NT)
    product = total_high[: 2 * KX] + total_high[2 * KX :] + total_low
    out_ref[0, :KX, :] = product[:KX, :LANES] - product[KX:, LANES:]
    out_ref[0, KX:, :] = product[:KX, LANES:] + product[KX:, :LANES]


def fill_mix(waves_ref, factor_ref, energy_ref, mix_ref, group):
    wave_x = lax.broadcasted_iota(jnp.int32, (KX, LANES), 0)
    wave_y = waves_ref[group, 0:1, :]
    wave_z = waves_ref[group, 1:2, :]
    squared = wave_x * wave_x + jnp.broadcast_to(wave_y * wave_y + wave_z * wave_z, (KX, LANES))
    inside = (squared <= 1024) & (squared > 0)
    squared_f = squared.astype(jnp.float32)
    halving = jnp.where(wave_x == 0, jnp.float32(0.5), jnp.float32(1.0))
    weight = jnp.where(
        inside,
        halving * jnp.exp(-squared_f / 1600.0) / jnp.maximum(squared_f, 1.0),
        jnp.float32(0.0),
    )
    real = factor_ref[group, :KX, :]
    imag = factor_ref[group, KX:, :]
    energy = weight * (real * real + imag * imag)
    energy_ref[group] = sum(energy[i : i + 8] for i in range(0, KX, 8))
    g_real = weight * real
    g_imag = -weight * imag
    wave_y = wave_y.astype(jnp.float32)
    wave_z = wave_z.astype(jnp.float32)
    lanes_cos = slice(group * TILE, group * TILE + LANES)
    lanes_sin = slice(group * TILE + LANES, (group + 1) * TILE)
    for part, scale in enumerate((None, wave_y, wave_z)):
        re, im = (g_real, g_imag) if scale is None else (g_real * scale, g_imag * scale)
        for offset, cos_value, sin_value in ((0, re, -im), (KX, im, re)):
            at = slice(part * 2 * KX + offset, part * 2 * KX + offset + KX)
            low_at = slice(6 * KX + at.start, 6 * KX + at.stop)
            mix_ref[at, lanes_cos], mix_ref[low_at, lanes_cos] = split(cos_value)
            mix_ref[at, lanes_sin], mix_ref[low_at, lanes_sin] = split(sin_value)


def force_kernel(
    waves_ref, factor_ref, high_ref, low_ref, basis_ref, ions_ref, out_ref, energy_ref, mix_ref,
    *, force_scale, potential_scale,
):
    groups = factor_ref.shape[0]

    @pl.when(pl.program_id(0) == 0)
    def _():
        for group in range(groups):
            fill_mix(waves_ref, factor_ref, energy_ref, mix_ref, group)

    def matrix(ref):
        return jnp.concatenate([ref[:, i].reshape(groups * TILE, LANES) for i in range(2)], 1)

    by_high = dot(mix_ref[...], matrix(high_ref), NN)
    by_low = dot(mix_ref[: 6 * KX, :], matrix(low_ref), NN)
    total = by_high[: 6 * KX] + by_high[6 * KX :] + by_low
    re0, im0, rey, imy, rez, imz = (total[i * KX : (i + 1) * KX] for i in range(6))
    cos_part = basis_ref[:KX, :]
    sin_part = basis_ref[KX:, :]
    wave_x = lax.broadcasted_iota(jnp.int32, (KX, TILE), 0).astype(jnp.float32)

    def reduce(value):
        return jnp.sum(value, 0, keepdims=True)

    charge = ions_ref[3:4, :] * jnp.float32(force_scale)
    out_ref[0:1, :] = charge * reduce(wave_x * (re0 * sin_part + im0 * cos_part))
    out_ref[1:2, :] = charge * reduce(rey * sin_part + imy * cos_part)
    out_ref[2:3, :] = charge * reduce(rez * sin_part + imz * cos_part)
    out_ref[3:4, :] = jnp.float32(potential_scale) * reduce(re0 * cos_part - im0 * sin_part)


def tree_sum(parts):
    while len(parts) > 1:
        parts = [parts[i] + parts[i + 1] for i in range(0, len(parts), 2)]
    return parts[0]


def flip(value, axis, step):
    size = lax.axis_size(axis)
    return lax.ppermute(value, axis, [(i, i ^ step) for i in range(size)])


def swap_groups(value, step):
    return jnp.concatenate([value[i ^ step][None] for i in range(value.shape[0])], 0)


def whole(shape):
    return pl.BlockSpec(shape, lambda g: (0,) * len(shape))


def per_device(ions, col_ids):
    groups = lax.axis_size("kcol")
    ranks = lax.axis_size("ion")
    count = ions.shape[1]
    rows = count // LANES
    total = count * groups * ranks
    table_shape = ((SPAN + 1) * rows, LANES)
    tables = pl.pallas_call(
        table_kernel,
        out_shape=[jax.ShapeDtypeStruct(table_shape, jnp.float32)] * 4
        + [
            jax.ShapeDtypeStruct((2 * KX, count), jnp.float32),
            jax.ShapeDtypeStruct((4 * KX, count), jnp.bfloat16),
        ],
        scratch_shapes=[pltpu.VMEM((2, rows, LANES), jnp.float32)],
        name="tables",
    )(ions)
    *yz_tables, basis, left = tables

    cols = col_ids[None]
    step = 1
    while step < groups:
        cols = jnp.concatenate([cols, flip(cols, "kcol", step)], 0)
        step *= 2
    index = jnp.stack([cols // SPAN, cols % SPAN], 1)
    waves = index - HALF

    pick_spec = pl.BlockSpec((1, 2, LANES), lambda g: (g, 0, 0), memory_space=pltpu.SMEM)
    halves_shape = jax.ShapeDtypeStruct((groups, rows, TILE, LANES), jnp.bfloat16)
    halves_spec = pl.BlockSpec((1, rows, TILE, LANES), lambda g: (g, 0, 0, 0))
    partial_factor, high, low = pl.pallas_call(
        factor_kernel,
        grid=(groups,),
        in_specs=[pick_spec, *[whole(table_shape)] * 4, whole((4 * KX, count))],
        out_specs=[pl.BlockSpec((1, 2 * KX, LANES), lambda g: (g, 0, 0)), halves_spec, halves_spec],
        out_shape=[jax.ShapeDtypeStruct((groups, 2 * KX, LANES), jnp.float32), halves_shape, halves_shape],
        scratch_shapes=[pltpu.VMEM((LANES * rows, LANES), jnp.float32)] * 2,
        name="factor",
    )(index * rows, *yz_tables, left)

    pairs = partial_factor.reshape(groups // 2, 2, 2 * KX, LANES)
    kept = pairs[:, 0] + flip(pairs[:, 1], "kcol", 1)
    step = 2
    while step < groups:
        kept = kept + swap_groups(flip(kept, "kcol", step), step // 2)
        step *= 2
    step = 1
    while step < ranks:
        kept = kept + flip(kept, "ion", step)
        step *= 2
    factor = jnp.stack([kept, flip(kept, "kcol", 1)], 1).reshape(groups, 2 * KX, LANES)

    tile_spec = pl.BlockSpec((groups, 2, TILE, LANES), lambda t: (0, t, 0, 0))
    forces, energy_parts = pl.pallas_call(
        functools.partial(
            force_kernel,
            force_scale=0.04 * math.pi / math.sqrt(total),
            potential_scale=0.4 / math.sqrt(total),
        ),
        grid=(count // TILE,),
        in_specs=[
            whole(waves.shape),
            whole(factor.shape),
            tile_spec,
            tile_spec,
            pl.BlockSpec((2 * KX, TILE), lambda t: (0, t)),
            pl.BlockSpec((4, TILE), lambda t: (0, t)),
        ],
        out_specs=[pl.BlockSpec((4, TILE), lambda t: (0, t)), whole((groups, 8, LANES))],
        out_shape=[
            jax.ShapeDtypeStruct((4, count), jnp.float32),
            jax.ShapeDtypeStruct((groups, 8, LANES), jnp.float32),
        ],
        scratch_shapes=[pltpu.VMEM((12 * KX, groups * TILE), jnp.bfloat16)],
        name="force",
    )(waves, factor, high, low, basis, ions)
    energy = jnp.float32(0.01 / total) * jnp.sum(tree_sum([energy_parts[i] for i in range(groups)]))
    return (forces, energy)


def solution(mesh):
    return jax.shard_map(
        per_device,
        mesh=mesh,
        in_specs=(P(None, ("kcol", "ion")), P("kcol")),
        out_specs=(P(None, ("kcol", "ion")), P()),
        check_vma=False,
    )
```

```python
import functools
import math

import jax
import jax.numpy as jnp
from jax import lax
from jax.experimental import pallas as pl
from jax.experimental.pallas import tpu as pltpu
from jax.sharding import PartitionSpec as P

KX = 32
SPAN = 64
HALF = SPAN // 2
LANES = 128
TILE = 256
MIB = 1 << 20
NT = ((1,), (1,))
NN = ((1,), (0,))
SIN_COEFFS = (3.1415902702069918, -5.167406733272337, 2.5440105185033337, -0.5594624554679438)
COS_COEFFS = (0.9999999532476085, -4.934792830619664, 4.058411352862771, -1.3318765680813944, 0.21968961109803095)


def horner(coeffs, square):
    value = jnp.float32(coeffs[-1])
    for coeff in coeffs[-2::-1]:
        value = value * square + jnp.float32(coeff)
    return value


def cos_sin_turns(turns):
    rest = turns - jnp.round(turns)
    square = rest * rest
    sin_half = rest * horner(SIN_COEFFS, square)
    cos_half = horner(COS_COEFFS, square)
    twice = sin_half + sin_half
    return 1.0 - twice * sin_half, twice * cos_half


def split(value):
    high = value.astype(jnp.bfloat16)
    low = (value - high.astype(jnp.float32)).astype(jnp.bfloat16)
    return high, low


def dot(a, b, dims):
    return lax.dot_general(a, b, (dims, ((), ())), preferred_element_type=jnp.float32)


def row_starts(rows):
    return sorted({*range(0, rows - 7, 8), rows - 8})


def table_kernel(ions_ref, cos_y, sin_y, cos_z, sin_z, basis_ref, left_ref, coord_ref):
    count = ions_ref.shape[1]
    rows = count // LANES
    for s in range(rows):
        at = slice(s * LANES, (s + 1) * LANES)
        coord_ref[0, s : s + 1, :] = ions_ref[1:2, at]
        coord_ref[1, s : s + 1, :] = ions_ref[2:3, at]

    def fill(m, carry):
        wave = m.astype(jnp.float32)
        for axis, (cos_ref, sin_ref) in enumerate(((cos_y, sin_y), (cos_z, sin_z))):
            cos_part, sin_part = cos_sin_turns(coord_ref[axis] * wave)
            up = pl.ds((HALF + m) * rows, rows)
            down = pl.ds((HALF - m) * rows, rows)
            cos_ref[up, :] = cos_part
            sin_ref[up, :] = sin_part
            cos_ref[down, :] = cos_part
            sin_ref[down, :] = -sin_part
        return carry

    lax.fori_loop(0, HALF + 1, fill, 0)
    wave_x = lax.broadcasted_iota(jnp.int32, (KX, LANES), 0).astype(jnp.float32)

    def body(b, carry):
        at = pl.ds(pl.multiple_of(b * LANES, LANES), LANES)
        cos_part, sin_part = cos_sin_turns(wave_x * ions_ref[0:1, at])
        basis_ref[:KX, at] = cos_part
        basis_ref[KX:, at] = sin_part
        charge = ions_ref[3:4, at]
        left_ref[:KX, at], left_ref[2 * KX : 3 * KX, at] = split(charge * cos_part)
        left_ref[KX : 2 * KX, at], left_ref[3 * KX :, at] = split(charge * sin_part)
        return carry

    lax.fori_loop(0, rows, body, 0)


def factor_kernel(pick_ref, cos_y, sin_y, cos_z, sin_z, left_ref, out_ref, high_ref, low_ref, cos_ref, sin_ref):
    rows = left_ref.shape[1] // LANES

    def column(c, carry):
        at_y = pick_ref[0, 0, c]
        at_z = pick_ref[0, 1, c]
        for start in row_starts(rows):
            y_at = pl.ds(at_y + start, 8)
            z_at = pl.ds(at_z + start, 8)
            cy, sy, cz, sz = cos_y[y_at, :], sin_y[y_at, :], cos_z[z_at, :], sin_z[z_at, :]
            at = pl.ds(c * rows + start, 8)
            cos_ref[at, :] = cy * cz - sy * sz
            sin_ref[at, :] = sy * cz + cy * sz
        return carry

    lax.fori_loop(0, LANES, column, 0, unroll=8)
    total_high = jnp.zeros((4 * KX, 2 * LANES), jnp.float32)
    total_low = jnp.zeros((2 * KX, 2 * LANES), jnp.float32)
    for tile in range(rows // 2):
        for s in (2 * tile, 2 * tile + 1):
            at = pl.ds(s, LANES, stride=rows)
            high_ref[0, s, :LANES, :], low_ref[0, s, :LANES, :] = split(cos_ref[at, :])
            high_ref[0, s, LANES:, :], low_ref[0, s, LANES:, :] = split(sin_ref[at, :])
        high = jnp.concatenate([high_ref[0, 2 * tile], high_ref[0, 2 * tile + 1]], 1)
        low = jnp.concatenate([low_ref[0, 2 * tile], low_ref[0, 2 * tile + 1]], 1)
        left = left_ref[:, tile * TILE : (tile + 1) * TILE]
        total_high += dot(left, high, NT)
        total_low += dot(left[: 2 * KX], low, NT)
    product = total_high[: 2 * KX] + total_high[2 * KX :] + total_low
    out_ref[0, :KX, :] = product[:KX, :LANES] - product[KX:, LANES:]
    out_ref[0, KX:, :] = product[:KX, LANES:] + product[KX:, :LANES]


def fill_mix(waves_ref, factor_ref, energy_ref, mix_ref, group):
    wave_x = lax.broadcasted_iota(jnp.int32, (KX, LANES), 0)
    wave_y = waves_ref[group, 0:1, :]
    wave_z = waves_ref[group, 1:2, :]
    squared = wave_x * wave_x + jnp.broadcast_to(wave_y * wave_y + wave_z * wave_z, (KX, LANES))
    inside = (squared <= 1024) & (squared > 0)
    squared_f = squared.astype(jnp.float32)
    halving = jnp.where(wave_x == 0, jnp.float32(0.5), jnp.float32(1.0))
    weight = jnp.where(
        inside,
        halving * jnp.exp(-squared_f / 1600.0) / jnp.maximum(squared_f, 1.0),
        jnp.float32(0.0),
    )
    real = factor_ref[group, :KX, :]
    imag = factor_ref[group, KX:, :]
    energy = weight * (real * real + imag * imag)
    energy_ref[group] = sum(energy[i : i + 8] for i in range(0, KX, 8))
    g_real = weight * real
    g_imag = -weight * imag
    wave_y = wave_y.astype(jnp.float32)
    wave_z = wave_z.astype(jnp.float32)
    lanes_cos = slice(group * TILE, group * TILE + LANES)
    lanes_sin = slice(group * TILE + LANES, (group + 1) * TILE)
    for part, scale in enumerate((None, wave_y, wave_z)):
        re, im = (g_real, g_imag) if scale is None else (g_real * scale, g_imag * scale)
        for offset, cos_value, sin_value in ((0, re, -im), (KX, im, re)):
            at = slice(part * 2 * KX + offset, part * 2 * KX + offset + KX)
            low_at = slice(6 * KX + at.start, 6 * KX + at.stop)
            mix_ref[at, lanes_cos], mix_ref[low_at, lanes_cos] = split(cos_value)
            mix_ref[at, lanes_sin], mix_ref[low_at, lanes_sin] = split(sin_value)


def force_kernel(
    waves_ref, factor_ref, high_ref, low_ref, basis_ref, ions_ref, out_ref, energy_ref, mix_ref,
    *, force_scale, potential_scale,
):
    groups = factor_ref.shape[0]

    @pl.when(pl.program_id(0) == 0)
    def _():
        for group in range(groups):
            fill_mix(waves_ref, factor_ref, energy_ref, mix_ref, group)

    def matrix(ref):
        return jnp.concatenate([ref[:, i].reshape(groups * TILE, LANES) for i in range(2)], 1)

    by_high = dot(mix_ref[...], matrix(high_ref), NN)
    by_low = dot(mix_ref[: 6 * KX, :], matrix(low_ref), NN)
    total = by_high[: 6 * KX] + by_high[6 * KX :] + by_low
    re0, im0, rey, imy, rez, imz = (total[i * KX : (i + 1) * KX] for i in range(6))
    cos_part = basis_ref[:KX, :]
    sin_part = basis_ref[KX:, :]
    wave_x = lax.broadcasted_iota(jnp.int32, (KX, TILE), 0).astype(jnp.float32)

    def reduce(value):
        return jnp.sum(value, 0, keepdims=True)

    charge = ions_ref[3:4, :] * jnp.float32(force_scale)
    out_ref[0:1, :] = charge * reduce(wave_x * (re0 * sin_part + im0 * cos_part))
    out_ref[1:2, :] = charge * reduce(rey * sin_part + imy * cos_part)
    out_ref[2:3, :] = charge * reduce(rez * sin_part + imz * cos_part)
    out_ref[3:4, :] = jnp.float32(potential_scale) * reduce(re0 * cos_part - im0 * sin_part)


def tree_sum(parts):
    while len(parts) > 1:
        parts = [parts[i] + parts[i + 1] for i in range(0, len(parts), 2)]
    return parts[0]


def flip(value, axis, step):
    size = lax.axis_size(axis)
    return lax.ppermute(value, axis, [(i, i ^ step) for i in range(size)])


def swap_groups(value, step):
    return jnp.concatenate([value[i ^ step][None] for i in range(value.shape[0])], 0)


def whole(shape):
    return pl.BlockSpec(shape, lambda g: (0,) * len(shape))


def per_device(ions, col_ids):
    groups = lax.axis_size("kcol")
    ranks = lax.axis_size("ion")
    count = ions.shape[1]
    rows = count // LANES
    total = count * groups * ranks
    table_shape = ((SPAN + 1) * rows, LANES)
    tables = pl.pallas_call(
        table_kernel,
        out_shape=[jax.ShapeDtypeStruct(table_shape, jnp.float32)] * 4
        + [
            jax.ShapeDtypeStruct((2 * KX, count), jnp.float32),
            jax.ShapeDtypeStruct((4 * KX, count), jnp.bfloat16),
        ],
        scratch_shapes=[pltpu.VMEM((2, rows, LANES), jnp.float32)],
        compiler_params=pltpu.CompilerParams(vmem_limit_bytes=8 * MIB),
        name="tables",
    )(ions)
    *yz_tables, basis, left = tables

    cols = col_ids[None]
    step = 1
    while step < groups:
        cols = jnp.concatenate([cols, flip(cols, "kcol", step)], 0)
        step *= 2
    index = jnp.stack([cols // SPAN, cols % SPAN], 1)
    waves = index - HALF

    pick_spec = pl.BlockSpec((1, 2, LANES), lambda g: (g, 0, 0), memory_space=pltpu.SMEM)
    halves_shape = jax.ShapeDtypeStruct((groups, rows, TILE, LANES), jnp.bfloat16)
    halves_spec = pl.BlockSpec((1, rows, TILE, LANES), lambda g: (g, 0, 0, 0))
    partial_factor, high, low = pl.pallas_call(
        factor_kernel,
        grid=(groups,),
        in_specs=[pick_spec, *[whole(table_shape)] * 4, whole((4 * KX, count))],
        out_specs=[pl.BlockSpec((1, 2 * KX, LANES), lambda g: (g, 0, 0)), halves_spec, halves_spec],
        out_shape=[jax.ShapeDtypeStruct((groups, 2 * KX, LANES), jnp.float32), halves_shape, halves_shape],
        scratch_shapes=[pltpu.VMEM((LANES * rows, LANES), jnp.float32)] * 2,
        compiler_params=pltpu.CompilerParams(vmem_limit_bytes=20 * MIB),
        name="factor",
    )(index * rows, *yz_tables, left)

    pairs = partial_factor.reshape(groups // 2, 2, 2 * KX, LANES)
    kept = pairs[:, 0] + flip(pairs[:, 1], "kcol", 1)
    step = 2
    while step < groups:
        kept = kept + swap_groups(flip(kept, "kcol", step), step // 2)
        step *= 2
    step = 1
    while step < ranks:
        kept = kept + flip(kept, "ion", step)
        step *= 2
    factor = jnp.stack([kept, flip(kept, "kcol", 1)], 1).reshape(groups, 2 * KX, LANES)

    tile_spec = pl.BlockSpec((groups, 2, TILE, LANES), lambda t: (0, t, 0, 0))
    forces, energy_parts = pl.pallas_call(
        functools.partial(
            force_kernel,
            force_scale=0.04 * math.pi / math.sqrt(total),
            potential_scale=0.4 / math.sqrt(total),
        ),
        grid=(count // TILE,),
        in_specs=[
            whole(waves.shape),
            whole(factor.shape),
            tile_spec,
            tile_spec,
            pl.BlockSpec((2 * KX, TILE), lambda t: (0, t)),
            pl.BlockSpec((4, TILE), lambda t: (0, t)),
        ],
        out_specs=[pl.BlockSpec((4, TILE), lambda t: (0, t)), whole((groups, 8, LANES))],
        out_shape=[
            jax.ShapeDtypeStruct((4, count), jnp.float32),
            jax.ShapeDtypeStruct((groups, 8, LANES), jnp.float32),
        ],
        scratch_shapes=[pltpu.VMEM((12 * KX, groups * TILE), jnp.bfloat16)],
        compiler_params=pltpu.CompilerParams(vmem_limit_bytes=16 * MIB),
        name="force",
    )(waves, factor, high, low, basis, ions)
    energy = jnp.float32(0.01 / total) * jnp.sum(tree_sum([energy_parts[i] for i in range(groups)]))
    return (forces, energy)


def solution(mesh):
    return jax.shard_map(
        per_device,
        mesh=mesh,
        in_specs=(P(None, ("kcol", "ion")), P("kcol")),
        out_specs=(P(None, ("kcol", "ion")), P()),
        check_vma=False,
    )
```

```python
import functools
import math

import jax
import jax.numpy as jnp
from jax import lax
from jax.experimental import pallas as pl
from jax.experimental.pallas import tpu as pltpu
from jax.sharding import PartitionSpec as P

KX = 32
SPAN = 64
HALF = SPAN // 2
LANES = 128
TILE = 256
MIB = 1 << 20
NT = ((1,), (1,))
NN = ((1,), (0,))
SIN_COEFFS = (
    3.1415926401307073,
    -5.167710083507923,
    2.5500775232148563,
    -0.5982912856211671,
    0.07765766030589402,
)
COS_COEFFS = (
    0.9999999532476085,
    -4.934792830619664,
    4.058411352862771,
    -1.3318765680813944,
    0.21968961109803095,
)


def horner(coeffs, square):
    value = jnp.float32(coeffs[-1])
    for coeff in coeffs[-2::-1]:
        value = value * square + jnp.float32(coeff)
    return value


def cos_sin_turns(turns):
    rest = turns - jnp.round(turns)
    square = rest * rest
    sin_half = rest * horner(SIN_COEFFS, square)
    cos_half = horner(COS_COEFFS, square)
    twice = sin_half + sin_half
    return 1.0 - twice * sin_half, twice * cos_half


def times(a, b):
    return a[0] * b[0] - a[1] * b[1], a[1] * b[0] + a[0] * b[1]


def split(value):
    high = value.astype(jnp.bfloat16)
    low = (value - high.astype(jnp.float32)).astype(jnp.bfloat16)
    return high, low


def dot(a, b, dims):
    return lax.dot_general(a, b, (dims, ((), ())), preferred_element_type=jnp.float32)


def row_starts(rows):
    return sorted({*range(0, rows - 7, 8), rows - 8})


def fill_yz_tables(ions_ref, coord_ref, tables):
    rows = ions_ref.shape[1] // LANES
    for s in range(rows):
        at = slice(s * LANES, (s + 1) * LANES)
        coord_ref[0, s : s + 1, :] = ions_ref[1:2, at]
        coord_ref[1, s : s + 1, :] = ions_ref[2:3, at]
    for axis in range(2):
        for start in row_starts(rows):
            base = cos_sin_turns(coord_ref[axis, start : start + 8, :])
            value = (jnp.ones_like(base[0]), jnp.zeros_like(base[0]))
            for m in range(HALF + 1):
                up = 2 * (HALF + m) * rows + start
                down = 2 * (HALF - m) * rows + start
                if m < HALF:
                    tables[axis][up : up + 8, :] = value[0]
                    tables[axis][up + rows : up + rows + 8, :] = value[1]
                if m:
                    tables[axis][down : down + 8, :] = value[0]
                    tables[axis][down + rows : down + rows + 8, :] = -value[1]
                value = base if m == 0 else times(value, base)


def fill_x_tables(ions_ref, basis_ref, left_ref):
    rows = ions_ref.shape[1] // LANES
    wave = lax.broadcasted_iota(jnp.int32, (8, LANES), 0).astype(jnp.float32)
    for s in range(rows):
        at = slice(s * LANES, (s + 1) * LANES)
        coord = ions_ref[0:1, at]
        value = cos_sin_turns(wave * coord)
        stride = cos_sin_turns(jnp.broadcast_to(8.0 * coord, (8, LANES)))
        parts = [value]
        for _ in range(KX // 8 - 1):
            parts.append(times(parts[-1], stride))
        charge = ions_ref[3:4, at]
        for half in range(2):
            whole = jnp.concatenate([part[half] for part in parts], 0)
            basis_ref[half * KX : (half + 1) * KX, at] = whole
            high, low = split(charge * whole)
            left_ref[half * KX : (half + 1) * KX, at] = high
            left_ref[(2 + half) * KX : (3 + half) * KX, at] = low


def fill_columns(ids_ref, tables, phase_ref, columns):
    y_table, z_table = tables
    rows = phase_ref.shape[1] // LANES
    for c in columns:
        col = ids_ref[c]
        y_at = (col >> 6) * (2 * rows)
        z_at = (col & (SPAN - 1)) * (2 * rows)
        for start in row_starts(rows):
            y_part = [y_table[pl.ds(y_at + half * rows + start, 8), :] for half in range(2)]
            z_part = [z_table[pl.ds(z_at + half * rows + start, 8), :] for half in range(2)]
            at = pl.ds(c * rows + start, 8)
            phase_ref[0, at, :], phase_ref[1, at, :] = times(y_part, z_part)


def add_factors(left_ref, phase_ref, high_ref, low_ref, group, before_ref, out_ref, next_columns):
    rows = phase_ref.shape[1] // LANES
    tiles = rows // 2
    share = -(-LANES // tiles)
    by_high = jnp.zeros((4 * KX, TILE), jnp.float32)
    by_low = jnp.zeros((2 * KX, TILE), jnp.float32)
    for tile in range(tiles):
        pair = (2 * tile, 2 * tile + 1)
        for s in pair:
            for half in range(2):
                to = slice(half * LANES, (half + 1) * LANES)
                high, low = split(phase_ref[half, pl.ds(s, LANES, stride=rows), :])
                high_ref[group, s, to, :] = high
                low_ref[group, s, to, :] = low
        next_columns(range(tile * share, min((tile + 1) * share, LANES)))
        high = jnp.concatenate([high_ref[group, s] for s in pair], 1)
        low = jnp.concatenate([low_ref[group, s] for s in pair], 1)
        left = left_ref[:, tile * TILE : (tile + 1) * TILE]
        by_high += dot(left, high, NT)
        by_low += dot(left[: 2 * KX], low, NT)
    product = by_high[: 2 * KX] + by_high[2 * KX :] + by_low
    out_ref[group, :KX, :] = before_ref[group, :KX, :] + (product[:KX, :LANES] - product[KX:, LANES:])
    out_ref[group, KX:, :] = before_ref[group, KX:, :] + (product[:KX, LANES:] + product[KX:, :LANES])


def factor_kernel(
    ions_ref, ids0_ref, ids1_ref, before_ref, out_ref, high_ref, low_ref, basis_ref,
    coord_ref, left_ref, y_table, z_table, phase0_ref, phase1_ref,
):
    tables = (y_table, z_table)
    fill_yz_tables(ions_ref, coord_ref, tables)
    fill_x_tables(ions_ref, basis_ref, left_ref)

    def first_columns(step, carry):
        fill_columns(ids0_ref, tables, phase0_ref, [step * 16 + i for i in range(16)])
        return carry

    lax.fori_loop(0, LANES // 16, first_columns, 0)
    add_factors(
        left_ref, phase0_ref, high_ref, low_ref, 0, before_ref, out_ref,
        lambda columns: fill_columns(ids1_ref, tables, phase1_ref, columns),
    )
    add_factors(left_ref, phase1_ref, high_ref, low_ref, 1, before_ref, out_ref, lambda columns: None)


def mix_kernel(ids0_ref, ids1_ref, own_ref, other_ref, mix_ref, energy_ref):
    wave_x = lax.broadcasted_iota(jnp.int32, (KX, LANES), 0)
    halving = jnp.where(wave_x == 0, jnp.float32(0.5), jnp.float32(1.0))
    energies = []
    for group, (ids_ref, factor_ref) in enumerate(((ids0_ref, own_ref), (ids1_ref, other_ref))):
        wave_y = (ids_ref[...] >> 6) - HALF
        wave_z = (ids_ref[...] & (SPAN - 1)) - HALF
        squared = wave_x * wave_x + jnp.broadcast_to(wave_y * wave_y + wave_z * wave_z, (KX, LANES))
        inside = (squared <= 1024) & (squared > 0)
        squared_f = squared.astype(jnp.float32)
        weight = jnp.where(
            inside,
            halving * jnp.exp(-squared_f / 1600.0) / jnp.maximum(squared_f, 1.0),
            jnp.float32(0.0),
        )
        real = factor_ref[:KX, :]
        imag = factor_ref[KX:, :]
        energy = weight * (real * real + imag * imag)
        energies.append(sum(energy[i : i + 4] for i in range(0, KX, 4)))
        g_real = weight * real
        g_imag = -weight * imag
        lanes_cos = slice(group * TILE, group * TILE + LANES)
        lanes_sin = slice(group * TILE + LANES, (group + 1) * TILE)
        for part, wave in enumerate((None, wave_y, wave_z)):
            re, im = g_real, g_imag
            if wave is not None:
                re, im = re * wave.astype(jnp.float32), im * wave.astype(jnp.float32)
            for offset, cos_value, sin_value in ((0, re, -im), (KX, im, re)):
                at = slice(part * 2 * KX + offset, part * 2 * KX + offset + KX)
                low_at = slice(6 * KX + at.start, 6 * KX + at.stop)
                mix_ref[at, lanes_cos], mix_ref[low_at, lanes_cos] = split(cos_value)
                mix_ref[at, lanes_sin], mix_ref[low_at, lanes_sin] = split(sin_value)
    energy_ref[...] = energies[0] + energies[1]


def force_kernel(mix_ref, energy_ref, *refs, force_scale, potential_scale):
    *block_refs, out_ref = refs
    wave_x = lax.broadcasted_iota(jnp.int32, (KX, TILE), 0).astype(jnp.float32)

    def reduce(value):
        return jnp.sum(value, 0, keepdims=True)

    def matrix(ref, tile):
        return jnp.concatenate([ref[:, 2 * tile + i].reshape(2 * TILE, LANES) for i in range(2)], 1)

    for block in range(len(block_refs) // 4):
        high_ref, low_ref, basis_ref, ions_ref = block_refs[4 * block : 4 * block + 4]
        count = ions_ref.shape[1]
        for tile in range(count // TILE):
            at = slice(tile * TILE, (tile + 1) * TILE)
            to = slice(block * count + at.start, block * count + at.stop)
            by_high = dot(mix_ref[...], matrix(high_ref, tile), NN)
            by_low = dot(mix_ref[: 6 * KX, :], matrix(low_ref, tile), NN)
            total = by_high[: 6 * KX] + by_high[6 * KX :] + by_low
            re0, im0, rey, imy, rez, imz = (total[i * KX : (i + 1) * KX] for i in range(6))
            cos_part = basis_ref[:KX, at]
            sin_part = basis_ref[KX:, at]
            charge = ions_ref[3:4, at] * jnp.float32(force_scale)
            out_ref[0:1, to] = charge * reduce(wave_x * (re0 * sin_part + im0 * cos_part))
            out_ref[1:2, to] = charge * reduce(rey * sin_part + imy * cos_part)
            out_ref[2:3, to] = charge * reduce(rez * sin_part + imz * cos_part)
            out_ref[3:4, to] = jnp.float32(potential_scale) * reduce(re0 * cos_part - im0 * sin_part)
    out_ref[:, out_ref.shape[1] - LANES :] = energy_ref[...]


def flip(value, axis, step):
    size = lax.axis_size(axis)
    return lax.ppermute(value, axis, [(i, i ^ step) for i in range(size)])


def per_device(ions, col_ids):
    groups = lax.axis_size("kcol")
    ranks = lax.axis_size("ion")
    blocks = groups // 2
    count = ions.shape[1]
    rows = count // LANES
    total = count * groups * ranks

    ids = (col_ids, flip(col_ids, "kcol", 1))
    ion_blocks = [ions] + [flip(ions, "kcol", 2 * i) for i in range(1, blocks)]

    smem = pl.BlockSpec(memory_space=pltpu.SMEM)
    vmem = pl.BlockSpec(memory_space=pltpu.VMEM)
    params = pltpu.CompilerParams(vmem_limit_bytes=24 * MIB)
    halves_shape = jax.ShapeDtypeStruct((2, rows, TILE, LANES), jnp.bfloat16)
    factor_call = pl.pallas_call(
        factor_kernel,
        in_specs=[vmem, smem, smem, vmem],
        out_specs=[vmem] * 4,
        out_shape=[
            jax.ShapeDtypeStruct((2, 2 * KX, LANES), jnp.float32),
            halves_shape,
            halves_shape,
            jax.ShapeDtypeStruct((2 * KX, count), jnp.float32),
        ],
        scratch_shapes=[
            pltpu.VMEM((2, rows, LANES), jnp.float32),
            pltpu.VMEM((4 * KX, count), jnp.bfloat16),
            *[pltpu.VMEM((2 * (SPAN + 1) * rows, LANES), jnp.float32)] * 2,
            *[pltpu.VMEM((2, LANES * rows, LANES), jnp.float32)] * 2,
        ],
        compiler_params=params,
        name="factor",
    )
    partial_factor = jnp.zeros((2, 2 * KX, LANES), jnp.float32)
    saved = []
    for block in ion_blocks:
        partial_factor, high, low, basis = factor_call(block, *ids, partial_factor)
        saved.append((high, low, basis, block))

    own = partial_factor[0] + flip(partial_factor[1], "kcol", 1)
    step = 1
    while step < ranks:
        own = own + flip(own, "ion", step)
        step *= 2
    mix, energy = pl.pallas_call(
        mix_kernel,
        in_specs=[vmem] * 4,
        out_specs=[vmem] * 2,
        out_shape=[
            jax.ShapeDtypeStruct((12 * KX, 2 * TILE), jnp.bfloat16),
            jax.ShapeDtypeStruct((4, LANES), jnp.float32),
        ],
        compiler_params=params,
        name="mix",
    )(*[part.reshape(1, LANES) for part in ids], own, flip(own, "kcol", 1))

    def forces_of(parts, energy):
        return pl.pallas_call(
            functools.partial(
                force_kernel,
                force_scale=0.04 * math.pi / math.sqrt(total),
                potential_scale=0.4 / math.sqrt(total),
            ),
            in_specs=[vmem] * (2 + 4 * len(parts)),
            out_specs=vmem,
            out_shape=jax.ShapeDtypeStruct((4, len(parts) * count + LANES), jnp.float32),
            compiler_params=params,
            name="force",
        )(mix, energy, *[array for part in parts for array in part])

    received = []

    def with_received(first, last):
        value = forces_of(saved[first:last], energy)
        for array in received:
            tail = array[:, array.shape[1] - LANES :]
            value = value + jnp.concatenate([array[:, first * count : last * count], tail], 1)
        return value

    size = blocks // 2
    while size:
        received.append(flip(with_received(size, 2 * size), "kcol", 2 * size))
        size //= 2
    result = with_received(0, 1)
    return result[:, :count], jnp.float32(0.01 / total) * jnp.sum(result[:, count:])


def solution(mesh):
    return jax.shard_map(
        per_device,
        mesh=mesh,
        in_specs=(P(None, ("kcol", "ion")), P("kcol")),
        out_specs=(P(None, ("kcol", "ion")), P()),
        check_vma=False,
    )
```

```python
import functools
import math

import jax
import jax.numpy as jnp
from jax import lax
from jax.experimental import pallas as pl
from jax.experimental.pallas import tpu as pltpu
from jax.sharding import PartitionSpec as P

KX = 32
SPAN = 64
HALF = SPAN // 2
LANES = 128
TILE = 256
MIB = 1 << 20
NT = ((1,), (1,))
NN = ((1,), (0,))
SIN_COEFFS = (
    3.1415926401307073,
    -5.167710083507923,
    2.5500775232148563,
    -0.5982912856211671,
    0.07765766030589402,
)
COS_COEFFS = (
    0.9999999532476085,
    -4.934792830619664,
    4.058411352862771,
    -1.3318765680813944,
    0.21968961109803095,
)


def horner(coeffs, square):
    value = jnp.float32(coeffs[-1])
    for coeff in coeffs[-2::-1]:
        value = value * square + jnp.float32(coeff)
    return value


def cos_sin_turns(turns):
    rest = turns - jnp.round(turns)
    square = rest * rest
    sin_half = rest * horner(SIN_COEFFS, square)
    cos_half = horner(COS_COEFFS, square)
    twice = sin_half + sin_half
    return 1.0 - twice * sin_half, twice * cos_half


def times(a, b):
    return a[0] * b[0] - a[1] * b[1], a[1] * b[0] + a[0] * b[1]


def split(value):
    high = value.astype(jnp.bfloat16)
    low = (value - high.astype(jnp.float32)).astype(jnp.bfloat16)
    return high, low


def dot(a, b, dims):
    return lax.dot_general(a, b, (dims, ((), ())), preferred_element_type=jnp.float32)


def row_starts(rows):
    return sorted({*range(0, rows - 7, 8), rows - 8})


def yz_table_pieces(ions_ref, coord_ref, tables):
    rows = ions_ref.shape[1] // LANES

    def piece(axis, start):
        for s in range(start, start + 8):
            coord_ref[axis, s : s + 1, :] = ions_ref[1 + axis : 2 + axis, s * LANES : (s + 1) * LANES]
        base = cos_sin_turns(coord_ref[axis, start : start + 8, :])
        value = (jnp.ones_like(base[0]), jnp.zeros_like(base[0]))
        for m in range(HALF + 1):
            up = 2 * (HALF + m) * rows + start
            down = 2 * (HALF - m) * rows + start
            if m < HALF:
                tables[axis][up : up + 8, :] = value[0]
                tables[axis][up + rows : up + rows + 8, :] = value[1]
            if m:
                tables[axis][down : down + 8, :] = value[0]
                tables[axis][down + rows : down + rows + 8, :] = -value[1]
            value = base if m == 0 else times(value, base)

    return [functools.partial(piece, axis, start) for start in row_starts(rows) for axis in range(2)]


def x_table_pieces(ions_ref, basis_ref, left_ref):
    rows = ions_ref.shape[1] // LANES
    wave = lax.broadcasted_iota(jnp.int32, (8, LANES), 0).astype(jnp.float32)

    def piece(s):
        at = slice(s * LANES, (s + 1) * LANES)
        coord = ions_ref[0:1, at]
        value = cos_sin_turns(wave * coord)
        stride = cos_sin_turns(jnp.broadcast_to(8.0 * coord, (8, LANES)))
        parts = [value]
        for _ in range(KX // 8 - 1):
            parts.append(times(parts[-1], stride))
        charge = ions_ref[3:4, at]
        for half in range(2):
            whole = jnp.concatenate([part[half] for part in parts], 0)
            basis_ref[half * KX : (half + 1) * KX, at] = whole
            high, low = split(charge * whole)
            left_ref[half * KX : (half + 1) * KX, at] = high
            left_ref[(2 + half) * KX : (3 + half) * KX, at] = low

    return [functools.partial(piece, s) for s in range(rows)]


def fill_columns(rows_ref, group, tables, phase_ref, columns):
    y_table, z_table = tables
    rows = phase_ref.shape[1] // LANES
    for c in columns:
        y_at = rows_ref[2 * group, c]
        z_at = rows_ref[2 * group + 1, c]
        for start in row_starts(rows):
            y_part = [y_table[pl.ds(y_at + half * rows + start, 8), :] for half in range(2)]
            z_part = [z_table[pl.ds(z_at + half * rows + start, 8), :] for half in range(2)]
            at = pl.ds(c * rows + start, 8)
            phase_ref[0, at, :], phase_ref[1, at, :] = times(y_part, z_part)


def add_factors(left_ref, phase_ref, high_ref, low_ref, group, work):
    rows = phase_ref.shape[1] // LANES
    tiles = rows // 2
    by_high = jnp.zeros((4 * KX, TILE), jnp.float32)
    by_low = jnp.zeros((2 * KX, TILE), jnp.float32)
    for tile in range(tiles + 1):
        if tile:
            pair = (2 * tile - 2, 2 * tile - 1)
            high = jnp.concatenate([high_ref[group, s] for s in pair], 1)
            low = jnp.concatenate([low_ref[group, s] for s in pair], 1)
            left = left_ref[:, (tile - 1) * TILE : tile * TILE]
            by_high += dot(left, high, NT)
            by_low += dot(left[: 2 * KX], low, NT)
        if tile < tiles:
            for s in (2 * tile, 2 * tile + 1):
                for half in range(2):
                    to = slice(half * LANES, (half + 1) * LANES)
                    high, low = split(phase_ref[half, pl.ds(s, LANES, stride=rows), :])
                    high_ref[group, s, to, :] = high
                    low_ref[group, s, to, :] = low
            for pieces in work:
                for piece in pieces[tile * len(pieces) // tiles : (tile + 1) * len(pieces) // tiles]:
                    piece()
    product = by_high[: 2 * KX] + by_high[2 * KX :] + by_low
    real = product[:KX, :LANES] - product[KX:, LANES:]
    imag = product[:KX, LANES:] + product[KX:, :LANES]
    return jnp.concatenate([real, imag], 0)


def factor_kernel(ids0_ref, ids1_ref, *refs, blocks, has_before):
    refs = list(refs)
    before_ref = refs.pop(0) if has_before else None
    ions = [refs.pop(0) for _ in range(blocks)]
    out_ref = refs.pop(0)
    outs = [[refs.pop(0) for _ in range(3)] for _ in range(blocks)]
    coord_ref, found_ref, rows_ref, sem = (refs.pop(0) for _ in range(4))
    sets = [[refs.pop(0) for _ in range(3)] for _ in range(min(blocks, 2))]
    phases = refs
    rows = ions[0].shape[1] // LANES
    for group, ids_ref in enumerate((ids0_ref, ids1_ref)):
        found_ref[2 * group : 2 * group + 1, :] = (ids_ref[...] >> 6) * (2 * rows)
        found_ref[2 * group + 1 : 2 * group + 2, :] = (ids_ref[...] & (SPAN - 1)) * (2 * rows)
    copy = pltpu.make_async_copy(found_ref, rows_ref, sem)
    copy.start()

    def tables_of(block):
        left_ref, *tables = sets[block % 2]
        return (
            yz_table_pieces(ions[block], coord_ref, tables),
            x_table_pieces(ions[block], outs[block][2], left_ref),
        )

    def columns_of(block, group):
        tables = sets[block % 2][1:]
        return [functools.partial(fill_columns, rows_ref, group, tables, phases[group], [c]) for c in range(LANES)]

    for pieces in tables_of(0):
        for piece in pieces:
            piece()

    copy.wait()

    def first_columns(step, carry):
        fill_columns(rows_ref, 0, sets[0][1:], phases[0], [step * 16 + i for i in range(16)])
        return carry

    lax.fori_loop(0, LANES // 16, first_columns, 0)
    for group in range(2):
        out_ref[group] = before_ref[group] if has_before else jnp.zeros_like(out_ref[group])
    for block in range(blocks):
        high_ref, low_ref, _ = outs[block]
        following = tables_of(block + 1) if block + 1 < blocks else ([], [])
        for group in range(2):
            if group == 0:
                work = [following[0], columns_of(block, 1)]
            elif block + 1 < blocks:
                work = [following[1], columns_of(block + 1, 0)]
            else:
                work = []

            @pl.when(rows_ref[0, block] >= 0)
            def _():
                out_ref[group] += add_factors(sets[block % 2][0], phases[group], high_ref, low_ref, group, work)


def mix_kernel(ids0_ref, ids1_ref, own_ref, other_ref, mix_ref, energy_ref):
    wave_x = lax.broadcasted_iota(jnp.int32, (KX, LANES), 0)
    halving = jnp.where(wave_x == 0, jnp.float32(0.5), jnp.float32(1.0))
    energies = []
    for group, (ids_ref, factor_ref) in enumerate(((ids0_ref, own_ref), (ids1_ref, other_ref))):
        wave_y = (ids_ref[...] >> 6) - HALF
        wave_z = (ids_ref[...] & (SPAN - 1)) - HALF
        squared = wave_x * wave_x + jnp.broadcast_to(wave_y * wave_y + wave_z * wave_z, (KX, LANES))
        inside = (squared <= 1024) & (squared > 0)
        squared_f = squared.astype(jnp.float32)
        weight = jnp.where(
            inside,
            halving * jnp.exp(-squared_f / 1600.0) / jnp.maximum(squared_f, 1.0),
            jnp.float32(0.0),
        )
        real = factor_ref[:KX, :]
        imag = factor_ref[KX:, :]
        energy = weight * (real * real + imag * imag)
        energies.append(sum(energy[i : i + 4] for i in range(0, KX, 4)))
        g_real = weight * real
        g_imag = -weight * imag
        lanes_cos = slice(group * TILE, group * TILE + LANES)
        lanes_sin = slice(group * TILE + LANES, (group + 1) * TILE)
        for part, wave in enumerate((None, wave_y, wave_z)):
            re, im = g_real, g_imag
            if wave is not None:
                re, im = re * wave.astype(jnp.float32), im * wave.astype(jnp.float32)
            for offset, cos_value, sin_value in ((0, re, -im), (KX, im, re)):
                at = slice(part * 2 * KX + offset, part * 2 * KX + offset + KX)
                low_at = slice(6 * KX + at.start, 6 * KX + at.stop)
                mix_ref[at, lanes_cos], mix_ref[low_at, lanes_cos] = split(cos_value)
                mix_ref[at, lanes_sin], mix_ref[low_at, lanes_sin] = split(sin_value)
    energy_ref[...] = energies[0] + energies[1]


def force_kernel(mix_ref, energy_ref, *refs, force_scale, potential_scale):
    *block_refs, out_ref = refs
    wave_x = lax.broadcasted_iota(jnp.int32, (KX, TILE), 0).astype(jnp.float32)

    def reduce(value):
        return jnp.sum(value, 0, keepdims=True)

    def matrix(ref, tile):
        return jnp.concatenate([ref[:, 2 * tile + i].reshape(2 * TILE, LANES) for i in range(2)], 1)

    for block in range(len(block_refs) // 4):
        high_ref, low_ref, basis_ref, ions_ref = block_refs[4 * block : 4 * block + 4]
        count = ions_ref.shape[1]
        for tile in range(count // TILE):
            at = slice(tile * TILE, (tile + 1) * TILE)
            to = slice(block * count + at.start, block * count + at.stop)
            by_high = dot(mix_ref[...], matrix(high_ref, tile), NN)
            by_low = dot(mix_ref[: 6 * KX, :], matrix(low_ref, tile), NN)
            total = by_high[: 6 * KX] + by_high[6 * KX :] + by_low
            re0, im0, rey, imy, rez, imz = (total[i * KX : (i + 1) * KX] for i in range(6))
            cos_part = basis_ref[:KX, at]
            sin_part = basis_ref[KX:, at]
            charge = ions_ref[3:4, at] * jnp.float32(force_scale)
            out_ref[0:1, to] = charge * reduce(wave_x * (re0 * sin_part + im0 * cos_part))
            out_ref[1:2, to] = charge * reduce(rey * sin_part + imy * cos_part)
            out_ref[2:3, to] = charge * reduce(rez * sin_part + imz * cos_part)
            out_ref[3:4, to] = jnp.float32(potential_scale) * reduce(re0 * cos_part - im0 * sin_part)
    out_ref[:, out_ref.shape[1] - LANES :] = energy_ref[...]


def flip(value, axis, step):
    size = lax.axis_size(axis)
    return lax.ppermute(value, axis, [(i, i ^ step) for i in range(size)])


def per_device(ions, col_ids):
    groups = lax.axis_size("kcol")
    ranks = lax.axis_size("ion")
    blocks = groups // 2
    count = ions.shape[1]
    rows = count // LANES
    total = count * groups * ranks

    ids = [part.reshape(1, LANES) for part in (col_ids, flip(col_ids, "kcol", 1))]
    ion_blocks = [ions] + [flip(ions, "kcol", 2 * i) for i in range(1, blocks)]

    vmem = pl.BlockSpec(memory_space=pltpu.VMEM)
    params = pltpu.CompilerParams(vmem_limit_bytes=24 * MIB)
    halves_shape = jax.ShapeDtypeStruct((2, rows, TILE, LANES), jnp.bfloat16)

    def factors_of(ion_blocks, before):
        number = len(ion_blocks)
        extra = [] if before is None else [before]
        sets = [
            pltpu.VMEM((4 * KX, count), jnp.bfloat16),
            *[pltpu.VMEM((2 * (SPAN + 1) * rows, LANES), jnp.float32)] * 2,
        ]
        out, *rest = pl.pallas_call(
            functools.partial(factor_kernel, blocks=number, has_before=before is not None),
            in_specs=[vmem] * (2 + number + len(extra)),
            out_specs=[vmem] * (1 + 3 * number),
            out_shape=[
                jax.ShapeDtypeStruct((2, 2 * KX, LANES), jnp.float32),
                *[halves_shape, halves_shape, jax.ShapeDtypeStruct((2 * KX, count), jnp.float32)] * number,
            ],
            scratch_shapes=[
                pltpu.VMEM((2, rows, LANES), jnp.float32),
                pltpu.VMEM((4, LANES), jnp.int32),
                pltpu.SMEM((4, LANES), jnp.int32),
                pltpu.SemaphoreType.DMA,
                *sets * min(number, 2),
                *[pltpu.VMEM((2, LANES * rows, LANES), jnp.float32)] * 2,
            ],
            compiler_params=params,
            name="factor",
        )(*ids, *extra, *ion_blocks)
        return out, [(*rest[3 * i : 3 * i + 3], ion_blocks[i]) for i in range(number)]

    partial_factor, saved = factors_of(ion_blocks[:1], None)
    for first in range(1, blocks, 3):
        partial_factor, more = factors_of(ion_blocks[first : first + 3], partial_factor)
        saved += more

    own = partial_factor[0] + flip(partial_factor[1], "kcol", 1)
    step = 1
    while step < ranks:
        own = own + flip(own, "ion", step)
        step *= 2
    mix, energy = pl.pallas_call(
        mix_kernel,
        in_specs=[vmem] * 4,
        out_specs=[vmem] * 2,
        out_shape=[
            jax.ShapeDtypeStruct((12 * KX, 2 * TILE), jnp.bfloat16),
            jax.ShapeDtypeStruct((4, LANES), jnp.float32),
        ],
        compiler_params=params,
        name="mix",
    )(*ids, own, flip(own, "kcol", 1))

    def forces_of(parts, energy):
        return pl.pallas_call(
            functools.partial(
                force_kernel,
                force_scale=0.04 * math.pi / math.sqrt(total),
                potential_scale=0.4 / math.sqrt(total),
            ),
            in_specs=[vmem] * (2 + 4 * len(parts)),
            out_specs=vmem,
            out_shape=jax.ShapeDtypeStruct((4, len(parts) * count + LANES), jnp.float32),
            compiler_params=params,
            name="force",
        )(mix, energy, *[array for part in parts for array in part])

    received = []

    def with_received(first, last):
        value = forces_of(saved[first:last], energy)
        for array in received:
            tail = array[:, array.shape[1] - LANES :]
            value = value + jnp.concatenate([array[:, first * count : last * count], tail], 1)
        return value

    size = blocks // 2
    while size:
        received.append(flip(with_received(size, 2 * size), "kcol", 2 * size))
        size //= 2
    result = with_received(0, 1)
    return result[:, :count], jnp.float32(0.01 / total) * jnp.sum(result[:, count:])


def solution(mesh):
    return jax.shard_map(
        per_device,
        mesh=mesh,
        in_specs=(P(None, ("kcol", "ion")), P("kcol")),
        out_specs=(P(None, ("kcol", "ion")), P()),
        check_vma=False,
    )
```

```python
import functools
import math

import jax
import jax.numpy as jnp
from jax import lax
from jax.experimental import pallas as pl
from jax.experimental.pallas import tpu as pltpu
from jax.sharding import PartitionSpec as P

KX = 32
SPAN = 64
HALF = SPAN // 2
LANES = 128
TILE = 256
MIB = 1 << 20
NT = ((1,), (1,))
NN = ((1,), (0,))
SIN_COEFFS = (
    3.1415926401307073,
    -5.167710083507923,
    2.5500775232148563,
    -0.5982912856211671,
    0.07765766030589402,
)
COS_COEFFS = (
    0.9999999532476085,
    -4.934792830619664,
    4.058411352862771,
    -1.3318765680813944,
    0.21968961109803095,
)


def horner(coeffs, square):
    value = jnp.float32(coeffs[-1])
    for coeff in coeffs[-2::-1]:
        value = value * square + jnp.float32(coeff)
    return value


def cos_sin_turns(turns):
    rest = turns - jnp.round(turns)
    square = rest * rest
    sin_half = rest * horner(SIN_COEFFS, square)
    cos_half = horner(COS_COEFFS, square)
    twice = sin_half + sin_half
    return 1.0 - twice * sin_half, twice * cos_half


def times(a, b):
    return a[0] * b[0] - a[1] * b[1], a[1] * b[0] + a[0] * b[1]


def split(value):
    high = value.astype(jnp.bfloat16)
    low = (value - high.astype(jnp.float32)).astype(jnp.bfloat16)
    return high, low


def dot(a, b, dims):
    return lax.dot_general(a, b, (dims, ((), ())), preferred_element_type=jnp.float32)


def row_starts(rows):
    return sorted({*range(0, rows - 7, 8), rows - 8})


def yz_table_pieces(ions_ref, coord_ref, tables):
    rows = ions_ref.shape[1] // LANES

    def piece(axis, start):
        for s in range(start, start + 8):
            coord_ref[axis, s : s + 1, :] = ions_ref[1 + axis : 2 + axis, s * LANES : (s + 1) * LANES]
        base = cos_sin_turns(coord_ref[axis, start : start + 8, :])
        value = (jnp.ones_like(base[0]), jnp.zeros_like(base[0]))
        for m in range(HALF + 1):
            up = 2 * (HALF + m) * rows + start
            down = 2 * (HALF - m) * rows + start
            if m < HALF:
                tables[axis][up : up + 8, :] = value[0]
                tables[axis][up + rows : up + rows + 8, :] = value[1]
            if m:
                tables[axis][down : down + 8, :] = value[0]
                tables[axis][down + rows : down + rows + 8, :] = -value[1]
            value = base if m == 0 else times(value, base)

    return [functools.partial(piece, axis, start) for start in row_starts(rows) for axis in range(2)]


def x_table_pieces(ions_ref, basis_ref, left_ref):
    rows = ions_ref.shape[1] // LANES
    wave = lax.broadcasted_iota(jnp.int32, (8, LANES), 0).astype(jnp.float32)

    def piece(s):
        at = slice(s * LANES, (s + 1) * LANES)
        coord = ions_ref[0:1, at]
        value = cos_sin_turns(wave * coord)
        stride = cos_sin_turns(jnp.broadcast_to(8.0 * coord, (8, LANES)))
        parts = [value]
        for _ in range(KX // 8 - 1):
            parts.append(times(parts[-1], stride))
        charge = ions_ref[3:4, at]
        for half in range(2):
            whole = jnp.concatenate([part[half] for part in parts], 0)
            basis_ref[half * KX : (half + 1) * KX, at] = whole
            high, low = split(charge * whole)
            left_ref[half * KX : (half + 1) * KX, at] = high
            left_ref[(2 + half) * KX : (3 + half) * KX, at] = low

    return [functools.partial(piece, s) for s in range(rows)]


def fill_columns(rows_ref, group, tables, phase_ref, columns):
    y_table, z_table = tables
    rows = phase_ref.shape[1] // LANES
    for c in columns:
        y_at = rows_ref[2 * group, c]
        z_at = rows_ref[2 * group + 1, c]
        for start in row_starts(rows):
            y_part = [y_table[pl.ds(y_at + half * rows + start, 8), :] for half in range(2)]
            z_part = [z_table[pl.ds(z_at + half * rows + start, 8), :] for half in range(2)]
            at = pl.ds(c * rows + start, 8)
            phase_ref[0, at, :], phase_ref[1, at, :] = times(y_part, z_part)


def fetch_kernel(ions_hbm, ids_hbm, ions_ref, ids_ref, y_table, z_table, coord_ref, sems):
    copies = [
        pltpu.make_async_copy(ions_hbm, ions_ref, sems.at[0]),
        pltpu.make_async_copy(ids_hbm, ids_ref, sems.at[1]),
    ]
    for copy in copies:
        copy.start()
    for copy in copies:
        copy.wait()
    for piece in yz_table_pieces(ions_ref, coord_ref, (y_table, z_table)):
        piece()


def add_factors(left_ref, phase_ref, high_ref, low_ref, group, work):
    rows = phase_ref.shape[1] // LANES
    tiles = rows // 2
    by_high = jnp.zeros((4 * KX, TILE), jnp.float32)
    by_low = jnp.zeros((2 * KX, TILE), jnp.float32)
    for tile in range(tiles + 1):
        if tile:
            pair = (2 * tile - 2, 2 * tile - 1)
            high = jnp.concatenate([high_ref[group, s] for s in pair], 1)
            low = jnp.concatenate([low_ref[group, s] for s in pair], 1)
            left = left_ref[:, (tile - 1) * TILE : tile * TILE]
            by_high += dot(left, high, NT)
            by_low += dot(left[: 2 * KX], low, NT)
        if tile < tiles:
            for s in (2 * tile, 2 * tile + 1):
                for half in range(2):
                    to = slice(half * LANES, (half + 1) * LANES)
                    high, low = split(phase_ref[half, pl.ds(s, LANES, stride=rows), :])
                    high_ref[group, s, to, :] = high
                    low_ref[group, s, to, :] = low
            for pieces in work:
                for piece in pieces[tile * len(pieces) // tiles : (tile + 1) * len(pieces) // tiles]:
                    piece()
    product = by_high[: 2 * KX] + by_high[2 * KX :] + by_low
    real = product[:KX, :LANES] - product[KX:, LANES:]
    imag = product[:KX, LANES:] + product[KX:, :LANES]
    return jnp.concatenate([real, imag], 0)


def factor_kernel(ids0_ref, ids1_ref, *refs, blocks, has_before):
    refs = list(refs)
    before_ref = refs.pop(0) if has_before else None
    given = [] if has_before else [refs.pop(0) for _ in range(2)]
    ions = [refs.pop(0) for _ in range(blocks)]
    out_ref = refs.pop(0)
    outs = [[refs.pop(0) for _ in range(3)] for _ in range(blocks)]
    coord_ref, found_ref, rows_ref, sem = (refs.pop(0) for _ in range(4))
    sets = [[refs.pop(0)] + given] if given else [[refs.pop(0) for _ in range(3)] for _ in range(min(blocks, 2))]
    phases = refs
    rows = ions[0].shape[1] // LANES
    for group, ids_ref in enumerate((ids0_ref, ids1_ref)):
        found_ref[2 * group : 2 * group + 1, :] = (ids_ref[...] >> 6) * (2 * rows)
        found_ref[2 * group + 1 : 2 * group + 2, :] = (ids_ref[...] & (SPAN - 1)) * (2 * rows)
    copy = pltpu.make_async_copy(found_ref, rows_ref, sem)
    copy.start()

    def tables_of(block):
        left_ref, *tables = sets[block % 2]
        return (
            yz_table_pieces(ions[block], coord_ref, tables),
            x_table_pieces(ions[block], outs[block][2], left_ref),
        )

    def columns_of(block, group):
        tables = sets[block % 2][1:]
        return [functools.partial(fill_columns, rows_ref, group, tables, phases[group], [c]) for c in range(LANES)]

    for pieces in tables_of(0)[len(given) // 2 :]:
        for piece in pieces:
            piece()

    copy.wait()

    def first_columns(step, carry):
        fill_columns(rows_ref, 0, sets[0][1:], phases[0], [step * 16 + i for i in range(16)])
        return carry

    lax.fori_loop(0, LANES // 16, first_columns, 0)
    for group in range(2):
        out_ref[group] = before_ref[group] if has_before else jnp.zeros_like(out_ref[group])
    for block in range(blocks):
        high_ref, low_ref, _ = outs[block]
        following = tables_of(block + 1) if block + 1 < blocks else ([], [])
        for group in range(2):
            if group == 0:
                work = [following[0], columns_of(block, 1)]
            elif block + 1 < blocks:
                work = [following[1], columns_of(block + 1, 0)]
            else:
                work = []

            @pl.when(rows_ref[0, block] >= 0)
            def _():
                out_ref[group] += add_factors(sets[block % 2][0], phases[group], high_ref, low_ref, group, work)


def mix_kernel(ids0_ref, ids1_ref, own_ref, other_ref, mix_ref, energy_ref):
    wave_x = lax.broadcasted_iota(jnp.int32, (KX, LANES), 0)
    halving = jnp.where(wave_x == 0, jnp.float32(0.5), jnp.float32(1.0))
    energies = []
    for group, (ids_ref, factor_ref) in enumerate(((ids0_ref, own_ref), (ids1_ref, other_ref))):
        wave_y = (ids_ref[...] >> 6) - HALF
        wave_z = (ids_ref[...] & (SPAN - 1)) - HALF
        squared = wave_x * wave_x + jnp.broadcast_to(wave_y * wave_y + wave_z * wave_z, (KX, LANES))
        inside = (squared <= 1024) & (squared > 0)
        squared_f = squared.astype(jnp.float32)
        weight = jnp.where(
            inside,
            halving * jnp.exp(-squared_f / 1600.0) / jnp.maximum(squared_f, 1.0),
            jnp.float32(0.0),
        )
        real = factor_ref[:KX, :]
        imag = factor_ref[KX:, :]
        energy = weight * (real * real + imag * imag)
        energies.append(sum(energy[i : i + 4] for i in range(0, KX, 4)))
        g_real = weight * real
        g_imag = -weight * imag
        lanes_cos = slice(group * TILE, group * TILE + LANES)
        lanes_sin = slice(group * TILE + LANES, (group + 1) * TILE)
        for part, wave in enumerate((None, wave_y, wave_z)):
            re, im = g_real, g_imag
            if wave is not None:
                re, im = re * wave.astype(jnp.float32), im * wave.astype(jnp.float32)
            for offset, cos_value, sin_value in ((0, re, -im), (KX, im, re)):
                at = slice(part * 2 * KX + offset, part * 2 * KX + offset + KX)
                low_at = slice(6 * KX + at.start, 6 * KX + at.stop)
                mix_ref[at, lanes_cos], mix_ref[low_at, lanes_cos] = split(cos_value)
                mix_ref[at, lanes_sin], mix_ref[low_at, lanes_sin] = split(sin_value)
    energy_ref[...] = energies[0] + energies[1]


def force_kernel(mix_ref, energy_ref, *refs, force_scale, potential_scale):
    *block_refs, out_ref = refs
    wave_x = lax.broadcasted_iota(jnp.int32, (KX, TILE), 0).astype(jnp.float32)

    def reduce(value):
        return jnp.sum(value, 0, keepdims=True)

    def matrix(ref, tile):
        return jnp.concatenate([ref[:, 2 * tile + i].reshape(2 * TILE, LANES) for i in range(2)], 1)

    for block in range(len(block_refs) // 4):
        high_ref, low_ref, basis_ref, ions_ref = block_refs[4 * block : 4 * block + 4]
        count = ions_ref.shape[1]
        for tile in range(count // TILE):
            at = slice(tile * TILE, (tile + 1) * TILE)
            to = slice(block * count + at.start, block * count + at.stop)
            by_high = dot(mix_ref[...], matrix(high_ref, tile), NN)
            by_low = dot(mix_ref[: 6 * KX, :], matrix(low_ref, tile), NN)
            total = by_high[: 6 * KX] + by_high[6 * KX :] + by_low
            re0, im0, rey, imy, rez, imz = (total[i * KX : (i + 1) * KX] for i in range(6))
            cos_part = basis_ref[:KX, at]
            sin_part = basis_ref[KX:, at]
            charge = ions_ref[3:4, at] * jnp.float32(force_scale)
            out_ref[0:1, to] = charge * reduce(wave_x * (re0 * sin_part + im0 * cos_part))
            out_ref[1:2, to] = charge * reduce(rey * sin_part + imy * cos_part)
            out_ref[2:3, to] = charge * reduce(rez * sin_part + imz * cos_part)
            out_ref[3:4, to] = jnp.float32(potential_scale) * reduce(re0 * cos_part - im0 * sin_part)
    out_ref[:, out_ref.shape[1] - LANES :] = energy_ref[...]


def last_kernel(value_ref, *refs, energy_scale):
    *received, out_ref, energy_ref = refs
    count = out_ref.shape[1]
    value = value_ref[:, :count]
    energy = value_ref[:, count:]
    for ref in received:
        value = value + ref[:, :count]
        energy = energy + ref[:, ref.shape[1] - LANES :]
    out_ref[...] = value
    energy_ref[0, 0] = jnp.float32(energy_scale) * jnp.sum(energy)


def flip(value, axis, step):
    size = lax.axis_size(axis)
    return lax.ppermute(value, axis, [(i, i ^ step) for i in range(size)])


def per_device(ions, col_ids):
    groups = lax.axis_size("kcol")
    ranks = lax.axis_size("ion")
    blocks = groups // 2
    count = ions.shape[1]
    rows = count // LANES
    total = count * groups * ranks

    def mask(i):
        return 2 * i | (i.bit_count() & 1)

    vmem = pl.BlockSpec(memory_space=pltpu.VMEM)
    hbm = pl.BlockSpec(memory_space=pltpu.HBM)
    params = pltpu.CompilerParams(vmem_limit_bytes=24 * MIB)
    own_ids = col_ids.reshape(1, LANES)
    other_ids = flip(own_ids, "kcol", 1)
    far_ions = [flip(ions, "kcol", mask(i)) for i in range(1, blocks)]
    near_ions, near_ids, *own_tables = pl.pallas_call(
        fetch_kernel,
        in_specs=[hbm, hbm],
        out_specs=[vmem] * 4,
        out_shape=[
            jax.ShapeDtypeStruct(ions.shape, jnp.float32),
            jax.ShapeDtypeStruct((1, LANES), jnp.int32),
            *[jax.ShapeDtypeStruct((2 * (SPAN + 1) * rows, LANES), jnp.float32)] * 2,
        ],
        scratch_shapes=[pltpu.VMEM((2, rows, LANES), jnp.float32), pltpu.SemaphoreType.DMA((2,))],
        compiler_params=params,
        name="fetch",
    )(ions, own_ids)
    ids = (near_ids, other_ids)
    ion_blocks = [near_ions, *far_ions]
    halves_shape = jax.ShapeDtypeStruct((2, rows, TILE, LANES), jnp.bfloat16)

    table_shape = (2 * (SPAN + 1) * rows, LANES)

    def factors_of(ion_blocks, before=None, tables=()):
        number = len(ion_blocks)
        extra = list(tables) if before is None else [before]
        left_shape = pltpu.VMEM((4 * KX, count), jnp.bfloat16)
        if tables:
            sets = [left_shape]
        else:
            sets = [left_shape, *[pltpu.VMEM(table_shape, jnp.float32)] * 2] * min(number, 2)
        out, *rest = pl.pallas_call(
            functools.partial(factor_kernel, blocks=number, has_before=before is not None),
            in_specs=[vmem] * (2 + number + len(extra)),
            out_specs=[vmem] * (1 + 3 * number),
            out_shape=[
                jax.ShapeDtypeStruct((2, 2 * KX, LANES), jnp.float32),
                *[halves_shape, halves_shape, jax.ShapeDtypeStruct((2 * KX, count), jnp.float32)] * number,
            ],
            scratch_shapes=[
                pltpu.VMEM((2, rows, LANES), jnp.float32),
                pltpu.VMEM((4, LANES), jnp.int32),
                pltpu.SMEM((4, LANES), jnp.int32),
                pltpu.SemaphoreType.DMA,
                *sets,
                *[pltpu.VMEM((2, LANES * rows, LANES), jnp.float32)] * 2,
            ],
            compiler_params=params,
            name="factor",
        )(*ids, *extra, *ion_blocks)
        return out, [(*rest[3 * i : 3 * i + 3], ion_blocks[i]) for i in range(number)]

    partial_factor, saved = factors_of(ion_blocks[:1], tables=own_tables)
    for first in range(1, blocks, 3):
        partial_factor, more = factors_of(ion_blocks[first : first + 3], partial_factor)
        saved += more

    own = partial_factor[0] + flip(partial_factor[1], "kcol", 1)
    step = 1
    while step < ranks:
        own = own + flip(own, "ion", step)
        step *= 2
    mix, energy = pl.pallas_call(
        mix_kernel,
        in_specs=[vmem] * 4,
        out_specs=[vmem] * 2,
        out_shape=[
            jax.ShapeDtypeStruct((12 * KX, 2 * TILE), jnp.bfloat16),
            jax.ShapeDtypeStruct((4, LANES), jnp.float32),
        ],
        compiler_params=params,
        name="mix",
    )(*ids, own, flip(own, "kcol", 1))

    def forces_of(parts, energy):
        return pl.pallas_call(
            functools.partial(
                force_kernel,
                force_scale=0.04 * math.pi / math.sqrt(total),
                potential_scale=0.4 / math.sqrt(total),
            ),
            in_specs=[vmem] * (2 + 4 * len(parts)),
            out_specs=vmem,
            out_shape=jax.ShapeDtypeStruct((4, len(parts) * count + LANES), jnp.float32),
            compiler_params=params,
            name="force",
        )(mix, energy, *[array for part in parts for array in part])

    received = []

    def with_received(first, last):
        value = forces_of(saved[first:last], energy)
        for array in received:
            tail = array[:, array.shape[1] - LANES :]
            value = value + jnp.concatenate([array[:, first * count : last * count], tail], 1)
        return value

    size = blocks // 2
    while size:
        received.append(flip(with_received(size, 2 * size), "kcol", mask(size)))
        size //= 2
    forces, energy_out = pl.pallas_call(
        functools.partial(last_kernel, energy_scale=0.01 / total),
        in_specs=[vmem] * (1 + len(received)),
        out_specs=[vmem, pl.BlockSpec(memory_space=pltpu.SMEM)],
        out_shape=[jax.ShapeDtypeStruct(ions.shape, jnp.float32), jax.ShapeDtypeStruct((1, 1), jnp.float32)],
        compiler_params=params,
        name="last",
    )(forces_of(saved[:1], energy), *received)
    return forces, energy_out.reshape(())


def solution(mesh):
    return jax.shard_map(
        per_device,
        mesh=mesh,
        in_specs=(P(None, ("kcol", "ion")), P("kcol")),
        out_specs=(P(None, ("kcol", "ion")), P()),
        check_vma=False,
    )
```

```python
import functools
import math

import jax
import jax.numpy as jnp
from jax import lax
from jax.experimental import pallas as pl
from jax.experimental.pallas import tpu as pltpu
from jax.sharding import PartitionSpec as P

KX = 32
SPAN = 64
HALF = SPAN // 2
LANES = 128
TILE = 256
MIB = 1 << 20
NT = ((1,), (1,))
NN = ((1,), (0,))
SIN_COEFFS = (
    3.1415926401307073,
    -5.167710083507923,
    2.5500775232148563,
    -0.5982912856211671,
    0.07765766030589402,
)
COS_COEFFS = (
    0.9999999532476085,
    -4.934792830619664,
    4.058411352862771,
    -1.3318765680813944,
    0.21968961109803095,
)


def horner(coeffs, square):
    value = jnp.float32(coeffs[-1])
    for coeff in coeffs[-2::-1]:
        value = value * square + jnp.float32(coeff)
    return value


def cos_sin_turns(turns):
    rest = turns - jnp.round(turns)
    square = rest * rest
    sin_half = rest * horner(SIN_COEFFS, square)
    cos_half = horner(COS_COEFFS, square)
    twice = sin_half + sin_half
    return 1.0 - twice * sin_half, twice * cos_half


def times(a, b):
    return a[0] * b[0] - a[1] * b[1], a[1] * b[0] + a[0] * b[1]


def split(value):
    high = value.astype(jnp.bfloat16)
    low = (value - high.astype(jnp.float32)).astype(jnp.bfloat16)
    return high, low


def dot(a, b, dims):
    return lax.dot_general(a, b, (dims, ((), ())), preferred_element_type=jnp.float32)


def row_starts(rows):
    return sorted({*range(0, rows - 7, 8), rows - 8})


def yz_table_pieces(ions_ref, coord_ref, tables):
    rows = ions_ref.shape[1] // LANES

    def piece(axis, start):
        for s in range(start, start + 8):
            coord_ref[axis, s : s + 1, :] = ions_ref[1 + axis : 2 + axis, s * LANES : (s + 1) * LANES]
        base = cos_sin_turns(coord_ref[axis, start : start + 8, :])
        value = (jnp.ones_like(base[0]), jnp.zeros_like(base[0]))
        for m in range(HALF + 1):
            up = 2 * (HALF + m) * rows + start
            down = 2 * (HALF - m) * rows + start
            if m < HALF:
                tables[axis][up : up + 8, :] = value[0]
                tables[axis][up + rows : up + rows + 8, :] = value[1]
            if m:
                tables[axis][down : down + 8, :] = value[0]
                tables[axis][down + rows : down + rows + 8, :] = -value[1]
            value = base if m == 0 else times(value, base)

    return [functools.partial(piece, axis, start) for start in row_starts(rows) for axis in range(2)]


def x_table_pieces(ions_ref, basis_ref, left_ref):
    rows = ions_ref.shape[1] // LANES
    wave = lax.broadcasted_iota(jnp.int32, (8, LANES), 0).astype(jnp.float32)

    def piece(s):
        at = slice(s * LANES, (s + 1) * LANES)
        coord = ions_ref[0:1, at]
        value = cos_sin_turns(wave * coord)
        stride = cos_sin_turns(jnp.broadcast_to(8.0 * coord, (8, LANES)))
        parts = [value]
        for _ in range(KX // 8 - 1):
            parts.append(times(parts[-1], stride))
        charge = ions_ref[3:4, at]
        for half in range(2):
            whole = jnp.concatenate([part[half] for part in parts], 0)
            basis_ref[half * KX : (half + 1) * KX, at] = whole
            high, low = split(charge * whole)
            left_ref[half * KX : (half + 1) * KX, at] = high
            left_ref[(2 + half) * KX : (3 + half) * KX, at] = low

    return [functools.partial(piece, s) for s in range(rows)]


def fill_columns(rows_ref, group, tables, phase_ref, columns):
    y_table, z_table = tables
    rows = phase_ref.shape[1] // LANES
    for c in columns:
        y_at = rows_ref[2 * group, c]
        z_at = rows_ref[2 * group + 1, c]
        for start in row_starts(rows):
            y_part = [y_table[pl.ds(y_at + half * rows + start, 8), :] for half in range(2)]
            z_part = [z_table[pl.ds(z_at + half * rows + start, 8), :] for half in range(2)]
            at = pl.ds(c * rows + start, 8)
            phase_ref[0, at, :], phase_ref[1, at, :] = times(y_part, z_part)


def fetch_kernel(ions_hbm, ids_hbm, ions_ref, ids_ref, y_table, z_table, coord_ref, sems):
    copies = [
        pltpu.make_async_copy(ions_hbm, ions_ref, sems.at[0]),
        pltpu.make_async_copy(ids_hbm, ids_ref, sems.at[1]),
    ]
    for copy in copies:
        copy.start()
    for copy in copies:
        copy.wait()
    for piece in yz_table_pieces(ions_ref, coord_ref, (y_table, z_table)):
        piece()


def order_ids(own_ref, other_ref):
    odd = jnp.broadcast_to(lax.axis_index("ion") & 1, own_ref.shape) == 1
    own, other = own_ref[...], other_ref[...]
    return jnp.where(odd, other, own), jnp.where(odd, own, other)


def add_factors(left_ref, phase_ref, high_ref, low_ref, group, work):
    rows = phase_ref.shape[1] // LANES
    tiles = rows // 2
    by_high = jnp.zeros((4 * KX, TILE), jnp.float32)
    by_low = jnp.zeros((2 * KX, TILE), jnp.float32)
    for tile in range(tiles):
        pair = (2 * tile, 2 * tile + 1)
        for s in pair:
            for half in range(2):
                to = slice(half * LANES, (half + 1) * LANES)
                high, low = split(phase_ref[half, pl.ds(s, LANES, stride=rows), :])
                high_ref[group, s, to, :] = high
                low_ref[group, s, to, :] = low
        for pieces in work:
            for piece in pieces[tile * len(pieces) // tiles : (tile + 1) * len(pieces) // tiles]:
                piece()
        high = jnp.concatenate([high_ref[group, s] for s in pair], 1)
        low = jnp.concatenate([low_ref[group, s] for s in pair], 1)
        left = left_ref[:, tile * TILE : (tile + 1) * TILE]
        by_high += dot(left, high, NT)
        by_low += dot(left[: 2 * KX], low, NT)
    product = by_high[: 2 * KX] + by_high[2 * KX :] + by_low
    real = product[:KX, :LANES] - product[KX:, LANES:]
    imag = product[:KX, LANES:] + product[KX:, :LANES]
    return jnp.concatenate([real, imag], 0)


def factor_kernel(ids0_ref, ids1_ref, *refs, blocks, has_before):
    refs = list(refs)
    before_ref = refs.pop(0) if has_before else None
    given = [] if has_before else [refs.pop(0) for _ in range(2)]
    ions = [refs.pop(0) for _ in range(blocks)]
    out_ref = refs.pop(0)
    outs = [[refs.pop(0) for _ in range(3)] for _ in range(blocks)]
    coord_ref, found_ref, rows_ref, sem = (refs.pop(0) for _ in range(4))
    sets = [[refs.pop(0)] + given] if given else [[refs.pop(0) for _ in range(3)] for _ in range(min(blocks, 2))]
    phases = refs
    rows = ions[0].shape[1] // LANES
    for group, ids in enumerate(order_ids(ids0_ref, ids1_ref)):
        found_ref[2 * group : 2 * group + 1, :] = (ids >> 6) * (2 * rows)
        found_ref[2 * group + 1 : 2 * group + 2, :] = (ids & (SPAN - 1)) * (2 * rows)
    copy = pltpu.make_async_copy(found_ref, rows_ref, sem)
    copy.start()

    def tables_of(block):
        left_ref, *tables = sets[block % 2]
        return (
            yz_table_pieces(ions[block], coord_ref, tables),
            x_table_pieces(ions[block], outs[block][2], left_ref),
        )

    def columns_of(block, group):
        tables = sets[block % 2][1:]
        return [functools.partial(fill_columns, rows_ref, group, tables, phases[group], [c]) for c in range(LANES)]

    for pieces in tables_of(0)[len(given) // 2 :]:
        for piece in pieces:
            piece()

    copy.wait()

    def first_columns(step, carry):
        fill_columns(rows_ref, 0, sets[0][1:], phases[0], [step * 16 + i for i in range(16)])
        return carry

    lax.fori_loop(0, LANES // 16, first_columns, 0)
    for group in range(2):
        out_ref[group] = before_ref[group] if has_before else jnp.zeros_like(out_ref[group])
    for block in range(blocks):
        high_ref, low_ref, _ = outs[block]
        following = tables_of(block + 1) if block + 1 < blocks else ([], [])
        for group in range(2):
            if group == 0:
                work = [following[0], columns_of(block, 1)]
            elif block + 1 < blocks:
                work = [following[1], columns_of(block + 1, 0)]
            else:
                work = []

            @pl.when(rows_ref[0, block] >= 0)
            def _():
                out_ref[group] += add_factors(sets[block % 2][0], phases[group], high_ref, low_ref, group, work)


def mix_kernel(ids0_ref, ids1_ref, own_ref, other_ref, mix_ref, energy_ref):
    wave_x = lax.broadcasted_iota(jnp.int32, (KX, LANES), 0)
    halving = jnp.where(wave_x == 0, jnp.float32(0.5), jnp.float32(1.0))
    energies = []
    for group, (ids, factor_ref) in enumerate(zip(order_ids(ids0_ref, ids1_ref), (own_ref, other_ref))):
        wave_y = (ids >> 6) - HALF
        wave_z = (ids & (SPAN - 1)) - HALF
        squared = wave_x * wave_x + jnp.broadcast_to(wave_y * wave_y + wave_z * wave_z, (KX, LANES))
        inside = (squared <= 1024) & (squared > 0)
        squared_f = squared.astype(jnp.float32)
        weight = jnp.where(
            inside,
            halving * jnp.exp(-squared_f / 1600.0) / jnp.maximum(squared_f, 1.0),
            jnp.float32(0.0),
        )
        real = factor_ref[:KX, :]
        imag = factor_ref[KX:, :]
        energy = weight * (real * real + imag * imag)
        energies.append(sum(energy[i : i + 4] for i in range(0, KX, 4)))
        g_real = weight * real
        g_imag = -weight * imag
        lanes_cos = slice(group * TILE, group * TILE + LANES)
        lanes_sin = slice(group * TILE + LANES, (group + 1) * TILE)
        for part, wave in enumerate((None, wave_y, wave_z)):
            re, im = g_real, g_imag
            if wave is not None:
                re, im = re * wave.astype(jnp.float32), im * wave.astype(jnp.float32)
            for offset, cos_value, sin_value in ((0, re, -im), (KX, im, re)):
                at = slice(part * 2 * KX + offset, part * 2 * KX + offset + KX)
                low_at = slice(6 * KX + at.start, 6 * KX + at.stop)
                mix_ref[at, lanes_cos], mix_ref[low_at, lanes_cos] = split(cos_value)
                mix_ref[at, lanes_sin], mix_ref[low_at, lanes_sin] = split(sin_value)
    energy_ref[...] = energies[0] + energies[1]


def force_kernel(mix_ref, energy_ref, *refs, force_scale, potential_scale):
    *block_refs, out_ref = refs
    wave_x = lax.broadcasted_iota(jnp.int32, (KX, TILE), 0).astype(jnp.float32)

    def reduce(value):
        return jnp.sum(value, 0, keepdims=True)

    def matrix(ref, tile):
        return jnp.concatenate([ref[:, 2 * tile + i].reshape(2 * TILE, LANES) for i in range(2)], 1)

    for block in range(len(block_refs) // 4):
        high_ref, low_ref, basis_ref, ions_ref = block_refs[4 * block : 4 * block + 4]
        count = ions_ref.shape[1]
        for tile in range(count // TILE):
            at = slice(tile * TILE, (tile + 1) * TILE)
            to = slice(block * count + at.start, block * count + at.stop)
            by_high = dot(mix_ref[...], matrix(high_ref, tile), NN)
            by_low = dot(mix_ref[: 6 * KX, :], matrix(low_ref, tile), NN)
            total = by_high[: 6 * KX] + by_high[6 * KX :] + by_low
            re0, im0, rey, imy, rez, imz = (total[i * KX : (i + 1) * KX] for i in range(6))
            cos_part = basis_ref[:KX, at]
            sin_part = basis_ref[KX:, at]
            charge = ions_ref[3:4, at] * jnp.float32(force_scale)
            out_ref[0:1, to] = charge * reduce(wave_x * (re0 * sin_part + im0 * cos_part))
            out_ref[1:2, to] = charge * reduce(rey * sin_part + imy * cos_part)
            out_ref[2:3, to] = charge * reduce(rez * sin_part + imz * cos_part)
            out_ref[3:4, to] = jnp.float32(potential_scale) * reduce(re0 * cos_part - im0 * sin_part)
    out_ref[:, out_ref.shape[1] - LANES :] = energy_ref[...]


def last_kernel(value_ref, *refs, energy_scale):
    *received, out_ref, energy_ref = refs
    count = out_ref.shape[1]
    value = value_ref[:, :count]
    energy = value_ref[:, count:]
    for ref in received:
        value = value + ref[:, :count]
        energy = energy + ref[:, ref.shape[1] - LANES :]
    out_ref[...] = value
    energy_ref[0, 0] = jnp.float32(energy_scale) * jnp.sum(energy)


def flip(value, axis, step):
    size = lax.axis_size(axis)
    return lax.ppermute(value, axis, [(i, i ^ step) for i in range(size)])


def permute(value, target):
    groups, ranks = lax.axis_size("kcol"), lax.axis_size("ion")
    pairs = []
    for k in range(groups):
        for z in range(ranks):
            to_k, to_z = target(k, z)
            pairs.append((k * ranks + z, to_k * ranks + to_z))
    return lax.ppermute(value, ("kcol", "ion"), pairs)


def per_device(ions, col_ids):
    groups = lax.axis_size("kcol")
    ranks = lax.axis_size("ion")
    blocks = groups // 2
    count = ions.shape[1]
    rows = count // LANES
    total = count * groups * ranks

    def mask(i):
        return 2 * i | (i.bit_count() & 1)

    vmem = pl.BlockSpec(memory_space=pltpu.VMEM)
    hbm = pl.BlockSpec(memory_space=pltpu.HBM)
    params = pltpu.CompilerParams(vmem_limit_bytes=24 * MIB)
    own_ids = col_ids.reshape(1, LANES)
    other_ids = flip(own_ids, "kcol", 1)
    far_ions = [flip(ions, "kcol", mask(i)) for i in range(1, blocks)]
    near_ions, near_ids, *own_tables = pl.pallas_call(
        fetch_kernel,
        in_specs=[hbm, hbm],
        out_specs=[vmem] * 4,
        out_shape=[
            jax.ShapeDtypeStruct(ions.shape, jnp.float32),
            jax.ShapeDtypeStruct((1, LANES), jnp.int32),
            *[jax.ShapeDtypeStruct((2 * (SPAN + 1) * rows, LANES), jnp.float32)] * 2,
        ],
        scratch_shapes=[pltpu.VMEM((2, rows, LANES), jnp.float32), pltpu.SemaphoreType.DMA((2,))],
        compiler_params=params,
        name="fetch",
    )(ions, own_ids)
    ids = (near_ids, other_ids)
    ion_blocks = [near_ions, *far_ions]
    halves_shape = jax.ShapeDtypeStruct((2, rows, TILE, LANES), jnp.bfloat16)

    table_shape = (2 * (SPAN + 1) * rows, LANES)

    def factors_of(ion_blocks, before=None, tables=()):
        number = len(ion_blocks)
        extra = list(tables) if before is None else [before]
        left_shape = pltpu.VMEM((4 * KX, count), jnp.bfloat16)
        if tables:
            sets = [left_shape]
        else:
            sets = [left_shape, *[pltpu.VMEM(table_shape, jnp.float32)] * 2] * min(number, 2)
        out, *rest = pl.pallas_call(
            functools.partial(factor_kernel, blocks=number, has_before=before is not None),
            in_specs=[vmem] * (2 + number + len(extra)),
            out_specs=[vmem] * (1 + 3 * number),
            out_shape=[
                jax.ShapeDtypeStruct((2, 2 * KX, LANES), jnp.float32),
                *[halves_shape, halves_shape, jax.ShapeDtypeStruct((2 * KX, count), jnp.float32)] * number,
            ],
            scratch_shapes=[
                pltpu.VMEM((2, rows, LANES), jnp.float32),
                pltpu.VMEM((4, LANES), jnp.int32),
                pltpu.SMEM((4, LANES), jnp.int32),
                pltpu.SemaphoreType.DMA,
                *sets,
                *[pltpu.VMEM((2, LANES * rows, LANES), jnp.float32)] * 2,
            ],
            compiler_params=params,
            name="factor",
        )(*ids, *extra, *ion_blocks)
        return out, [(*rest[3 * i : 3 * i + 3], ion_blocks[i]) for i in range(number)]

    partial_factor, saved = factors_of(ion_blocks[:1], tables=own_tables)
    for first in range(1, blocks, 3):
        partial_factor, more = factors_of(ion_blocks[first : first + 3], partial_factor)
        saved += more

    own = partial_factor[0] + flip(partial_factor[1], "kcol", 1)
    step = 1
    while step < ranks:
        own = own + permute(own, lambda k, z, step=step: (k ^ (step & 1), z ^ step))
        step *= 2
    mix, energy = pl.pallas_call(
        mix_kernel,
        in_specs=[vmem] * 4,
        out_specs=[vmem] * 2,
        out_shape=[
            jax.ShapeDtypeStruct((12 * KX, 2 * TILE), jnp.bfloat16),
            jax.ShapeDtypeStruct((4, LANES), jnp.float32),
        ],
        compiler_params=params,
        name="mix",
    )(*ids, own, flip(own, "kcol", 1))

    def forces_of(parts, energy):
        return pl.pallas_call(
            functools.partial(
                force_kernel,
                force_scale=0.04 * math.pi / math.sqrt(total),
                potential_scale=0.4 / math.sqrt(total),
            ),
            in_specs=[vmem] * (2 + 4 * len(parts)),
            out_specs=vmem,
            out_shape=jax.ShapeDtypeStruct((4, len(parts) * count + LANES), jnp.float32),
            compiler_params=params,
            name="force",
        )(mix, energy, *[array for part in parts for array in part])

    received = []

    def with_received(first, last):
        value = forces_of(saved[first:last], energy)
        for array in received:
            tail = array[:, array.shape[1] - LANES :]
            value = value + jnp.concatenate([array[:, first * count : last * count], tail], 1)
        return value

    size = blocks // 2
    while size:
        received.append(flip(with_received(size, 2 * size), "kcol", mask(size)))
        size //= 2
    forces, energy_out = pl.pallas_call(
        functools.partial(last_kernel, energy_scale=0.01 / total),
        in_specs=[vmem] * (1 + len(received)),
        out_specs=[vmem, pl.BlockSpec(memory_space=pltpu.SMEM)],
        out_shape=[jax.ShapeDtypeStruct(ions.shape, jnp.float32), jax.ShapeDtypeStruct((1, 1), jnp.float32)],
        compiler_params=params,
        name="last",
    )(forces_of(saved[:1], energy), *received)
    return forces, energy_out.reshape(())


def solution(mesh):
    return jax.shard_map(
        per_device,
        mesh=mesh,
        in_specs=(P(None, ("kcol", "ion")), P("kcol")),
        out_specs=(P(None, ("kcol", "ion")), P()),
        check_vma=False,
    )
```
